32 devices in a mesh: st: 8 (over y, x, core), hr: 4 (over z).
Axes of the slice: x: 2, y: 2, z: 4, core: 2. Of those that a mesh axis runs over, the one named last changes fastest.
Arguments:
- cotangent: bfloat16 [256, 64, 2048], P('hr', None, 'st'), may hold values from -24 to 24
- field: bfloat16 [256, 64, 2048], P('hr', None, 'st'), may hold values from -1.5 to 1.5
- temporal: bfloat16 [256, 256], replicated, may hold values from -0.375 to 0.375
- embed: float32 [16, 2048], P(None, 'st'), may hold values from -5 to 5
Outputs:
- field_grad: bfloat16 [256, 64, 2048], P('hr', None, 'st')
- embed_grad: float32 [16, 2048], P(None, 'st')
The draws below stay inside these ranges and needn't reach their ends.
All inputs are finite; a program needn't handle non-finite values.
Results may differ from the reference program's by a relative error of at most 0.02.
Values may be sent and summed in bfloat16 or wider, within the bound.
No kernel may reach another device: no remote copies, remote signals or barrier semaphores. Data moves between devices by JAX's collectives and lax.ppermute only.
A program may use at most 128 MiB of HBM per device.

```python
import math
import jax
import jax.numpy as jnp
from jax import lax

EMB = 16
CH = 64
T_SIZE = 256
NS = 2048


def draw_embed(key, part):
    group_key = jax.random.fold_in(key, 11)
    center_key = jax.random.fold_in(key, 12)
    offset_key = jax.random.fold_in(key, 13)
    station_order = jax.random.permutation(group_key, NS)
    cluster = station_order // 4
    centers = 2.5 * jax.random.normal(center_key, (EMB, NS // 4), jnp.float32)
    offsets = 0.5 * jax.random.normal(offset_key, (EMB, NS), jnp.float32)
    spread = jnp.take(centers, cluster, axis=1) + offsets
    return jnp.clip(spread, -5.0, 5.0)


def block_levels(stream_key, extent, cuts, low, top_value):
    def one(axis_at, parts):
        heights = jax.random.uniform(jax.random.fold_in(jax.random.fold_in(stream_key, 6), axis_at), (parts,), jnp.float32, low / len(cuts), top_value / len(cuts))
        return jnp.repeat(jnp.exp(heights), extent[axis_at] // parts).reshape((-1,) + (1,) * (len(extent) - axis_at - 1))

    loudness = one(*cuts[0])
    for cut in cuts[1:]:
        loudness = loudness * one(*cut)
    return loudness


def gaussian(key, shape, scale, most, split=(), kind=jnp.bfloat16):
    entries = scale * jax.random.normal(key, shape, jnp.float32)
    if split:
        entries = entries * block_levels(key, shape, split, -0.22, 0.18)
    return jnp.clip(entries, -most, most).astype(kind)


def setup_inputs(seed: int = 0) -> dict:
    key_list = jax.random.split(jax.random.key(seed), 5)
    cotangent = gaussian(key_list[0], (T_SIZE, CH, NS), 4.0, 24.0, ((0, 4), (2, 8)))
    field = gaussian(key_list[1], (T_SIZE, CH, NS), 0.25, 1.5, ((0, 4), (2, 8)))
    temporal = gaussian(key_list[2], (T_SIZE, T_SIZE), T_SIZE ** -0.5, 0.375)
    embed = draw_embed(jax.random.fold_in(key_list[4], 71), 0)
    return {"cotangent": cotangent, "field": field, "temporal": temporal, "embed": embed}


def reference(cotangent, field, temporal, embed):
    amplitude = 1.0 / math.sqrt(NS)
    cot_flat = cotangent.reshape(T_SIZE, CH * NS)
    mixed_cot = lax.dot_general(temporal, cot_flat, (((0,), (0,)), ((), ())), preferred_element_type=jnp.float32)
    mixed_cot = mixed_cot.astype(jnp.bfloat16).reshape(T_SIZE * CH, NS)
    sq_norm = lax.optimization_barrier(jnp.sum(embed * embed, axis=0))
    cross_term = jnp.dot(embed.T, embed, precision=lax.Precision.HIGHEST)
    distance = sq_norm[:, None] + sq_norm[None, :] - 2.0 * cross_term
    kernel = jnp.exp(distance * (-0.5 / EMB)) * amplitude
    kernel_bf = kernel.astype(jnp.bfloat16)
    field_grad = lax.dot_general(mixed_cot, kernel_bf, (((1,), (1,)), ((), ())), preferred_element_type=jnp.float32)
    field_grad = field_grad.astype(jnp.bfloat16).reshape(T_SIZE, CH, NS)
    gram = lax.dot_general(field.reshape(T_SIZE * CH, NS), mixed_cot, (((0,), (0,)), ((), ())), preferred_element_type=jnp.float32)
    weight = gram * kernel
    sym_weight = weight + weight.T
    embed_grad = jnp.dot(embed, sym_weight, precision=lax.Precision.HIGHEST) - embed * lax.optimization_barrier(jnp.sum(sym_weight, axis=0))[None, :]
    embed_grad = embed_grad * (1.0 / EMB)
    return (field_grad, embed_grad)
```

```python
import math

import jax
import jax.numpy as jnp
from jax import lax
from jax.experimental import pallas as pl
from jax.experimental.layout import Layout, with_layout_constraint
from jax.experimental.pallas import tpu as pltpu
from jax.sharding import PartitionSpec as P

HIGHEST = lax.Precision.HIGHEST
BF16 = jnp.bfloat16
F32 = jnp.float32
CHUNKS = 4

VMEM = pl.BlockSpec(memory_space=pltpu.VMEM)
SMEM = pl.BlockSpec(memory_space=pltpu.SMEM)


def row_major(x):
    return with_layout_constraint(x, Layout(major_to_minor=tuple(range(x.ndim))))


def kernel_tile(emb_left, emb_right, amplitude):
    cross_term = lax.dot_general(emb_left, emb_right, (((0,), (0,)), ((), ())), precision=HIGHEST)
    norm_left = jnp.sum(emb_left * emb_left, axis=0)
    norm_right = jnp.sum(emb_right * emb_right, axis=0)
    distance = norm_left[:, None] + norm_right[None, :] - 2.0 * cross_term
    return jnp.exp(distance * (-0.5 / emb_left.shape[0])) * amplitude


def cyclic(x, axis, size, shift):
    return lax.ppermute(x, axis, [(i, (i + shift) % size) for i in range(size)])


def flip(x, axis, size, mask):
    return lax.ppermute(x, axis, [(i, i ^ mask) for i in range(size)])


def mix_hours(mixer, pieces):
    peers = len(pieces)
    chans, hours, rows = pieces[0].shape

    def body(mixer_ref, *refs):
        ins, outs = refs[:peers], refs[peers:]
        for c in range(chans):
            whole = jnp.concatenate([r[c] for r in ins], axis=0)
            mixed = jnp.dot(mixer_ref[...], whole, preferred_element_type=F32).astype(BF16)
            for e in range(peers):
                outs[e][c] = mixed[e * hours : (e + 1) * hours]

    return pl.pallas_call(
        body,
        out_shape=[jax.ShapeDtypeStruct((chans, hours, rows), BF16)] * peers,
        in_specs=[VMEM] * (1 + peers),
        out_specs=[VMEM] * peers,
        name="mix_hours",
    )(mixer, *pieces)


def in_order(places, pieces):
    peers = len(pieces)
    chans, hours, rows = pieces[0].shape

    def body(places_ref, *refs):
        out = refs[peers]
        for e in range(peers):
            out[pl.ds(places_ref[e] * chans, chans)] = refs[e][...]

    return pl.pallas_call(
        body,
        out_shape=jax.ShapeDtypeStruct((peers * chans, hours, rows), BF16),
        in_specs=[SMEM] + [VMEM] * peers,
        out_specs=VMEM,
        name="in_order",
    )(places, *pieces)


def joined(refs, shape):
    out, at = [], 0
    for count in shape:
        parts = [r[...] for r in refs[at : at + count]]
        out.append(parts[0] if count == 1 else jnp.concatenate(parts, axis=0))
        at += count
    return out


def apply_kernel(ker_bf, parts, shape):
    total = len(parts)
    length = sum(p.shape[0] for p in parts[: shape[0]])
    width = parts[0].shape[1]

    def body(ker_ref, *refs):
        blocks = joined(refs[:total], shape)
        acc = None
        for q, block in enumerate(blocks):
            term = jnp.dot(
                block, ker_ref[q * width : (q + 1) * width, :], preferred_element_type=F32
            )
            acc = term if acc is None else acc + term
        refs[total][...] = acc[:, :width]
        refs[total + 1][...] = acc[:, width:].astype(BF16)

    return pl.pallas_call(
        body,
        out_shape=[
            jax.ShapeDtypeStruct((length, width), F32),
            jax.ShapeDtypeStruct((length, width), BF16),
        ],
        in_specs=[VMEM] * (1 + total),
        out_specs=[VMEM] * 2,
        name="apply_kernel",
    )(ker_bf, *parts)


def add_gram(gram, field_rows, parts, shape):
    total = len(parts)
    width = parts[0].shape[1]
    first = gram is None

    def body(*refs):
        if first:
            field_ref, out = refs[0], refs[-1]
            blocks = joined(refs[1 : 1 + total], shape)
        else:
            gram_ref, field_ref, out = refs[0], refs[1], refs[-1]
            blocks = joined(refs[2 : 2 + total], shape)
        for q, block in enumerate(blocks):
            term = jnp.dot(field_ref[...], block, preferred_element_type=F32)
            cols = slice(q * width, (q + 1) * width)
            out[:, cols] = term if first else gram_ref[:, cols] + term

    args = ([] if first else [gram]) + [field_rows] + list(parts)
    return pl.pallas_call(
        body,
        out_shape=jax.ShapeDtypeStruct((field_rows.shape[0], len(shape) * width), F32),
        in_specs=[VMEM] * len(args),
        out_specs=VMEM,
        input_output_aliases={} if first else {0: 0},
        name="add_gram",
    )(*args)


def gather_chips(block, stations):
    chips = stations // 2
    rows = block.shape[0]
    unit = 16
    parts_of = {0: [block]}
    for q in sorted(range(1, chips), key=lambda v: (bin(v).count("1"), v)):
        bits = [b for b in range(q.bit_length()) if q >> b & 1]
        if len(bits) == 1:
            parts_of[q] = [flip(block, "st", stations, 2 * q)]
            continue
        cuts = [rows // unit * a // len(bits) * unit for a in range(len(bits) + 1)]
        parts = []
        for a, b in enumerate(bits):
            source = parts_of[q ^ (1 << b)]
            source = source[0] if len(source) == 1 else jnp.concatenate(source, axis=0)
            parts.append(flip(source[cuts[a] : cuts[a + 1]], "st", stations, 2 << b))
        parts_of[q] = parts
    flat = [p for q in range(chips) for p in parts_of[q]]
    return flat, [len(parts_of[q]) for q in range(chips)]


def on_device(cotangent, field, temporal, embed):
    hours, chans, rows = cotangent.shape
    emb_width = embed.shape[0]
    stations = lax.axis_size("st")
    peers = lax.axis_size("hr")
    chips = stations // 2
    here = lax.axis_index("hr")
    amplitude = 1.0 / math.sqrt(rows * stations)
    group = chans // CHUNKS
    share = group // peers

    behind = [(here + peers - d) % peers for d in range(peers)]
    ahead = [(here + d) % peers for d in range(peers)]
    places = jnp.stack(behind).astype(jnp.int32)

    mixer = jnp.concatenate(
        [lax.dynamic_slice_in_dim(temporal, b * hours, hours, 0) for b in behind], axis=0
    )
    mixer = jnp.concatenate(
        [lax.dynamic_slice_in_dim(mixer, a * hours, hours, 1) for a in ahead], axis=1
    ).T

    def to_mixers(k, gate):
        turned = jnp.transpose(cotangent[:, k * group : (k + 1) * group], (1, 0, 2))
        turned = row_major(turned)
        if gate is not None:
            turned, _ = lax.optimization_barrier((turned, gate))
        pieces = [lax.dynamic_slice_in_dim(turned, a * share, share, 0) for a in ahead]
        return [p if d == 0 else cyclic(p, "hr", peers, d) for d, p in enumerate(pieces)]

    mixed = []
    for k in range(CHUNKS):
        gate = mixed[k - 2][0] if k >= 2 else None
        mixed.append(mix_hours(mixer, to_mixers(k, gate)))

    emb_partner = flip(embed, "st", stations, 1)
    emb_rows = jnp.concatenate([embed, emb_partner], axis=1)
    emb_cols = jnp.concatenate(
        [embed] + [flip(embed, "st", stations, 2 * q) for q in range(1, chips)], axis=1
    )
    ker = kernel_tile(emb_rows, emb_cols, amplitude)
    ker_bf = ker.astype(BF16).T

    field_rows = row_major(jnp.transpose(field, (2, 1, 0)).reshape(rows, chans * hours))
    field_rows = jnp.concatenate([field_rows, flip(field_rows, "st", stations, 1)], axis=0)

    gram = None
    outs = []
    for k in range(CHUNKS):
        back = [p if e == 0 else cyclic(p, "hr", peers, e) for e, p in enumerate(mixed[k])]
        block = in_order(places, back).reshape(group * hours, rows)
        parts, shape = gather_chips(block, stations)
        span = group * hours
        gram = add_gram(gram, field_rows[:, k * span : (k + 1) * span], parts, shape)
        own, other = apply_kernel(ker_bf, parts, shape)
        total = own + flip(other, "st", stations, 1).astype(F32)
        total = total.astype(BF16).reshape(group, hours, rows)
        outs.append(jnp.transpose(total, (1, 0, 2)))
    field_grad = jnp.concatenate(outs, axis=1)

    weight = gram * ker
    by_row = lax.dot_general(emb_cols, weight, (((1,), (1,)), ((), ())), precision=HIGHEST)
    by_row = by_row - emb_rows * jnp.sum(weight, axis=1)[None, :]
    by_col = jnp.dot(emb_rows, weight, precision=HIGHEST)
    by_col = by_col - emb_cols * jnp.sum(weight, axis=0)[None, :]
    scale = 1.0 / emb_width
    by_row = by_row * scale
    by_col = by_col * scale
    part = by_row[:, :rows] + by_col[:, :rows] + flip(by_row[:, rows:], "st", stations, 1)
    for q in range(1, chips):
        part = part + flip(by_col[:, q * rows : (q + 1) * rows], "st", stations, 2 * q)
    embed_grad = part
    for d in range(1, peers):
        embed_grad = embed_grad + cyclic(part, "hr", peers, d)
    return (field_grad, embed_grad)


def solution(mesh):
    return jax.shard_map(
        on_device,
        mesh=mesh,
        in_specs=(P("hr", None, "st"), P("hr", None, "st"), P(), P(None, "st")),
        out_specs=(P("hr", None, "st"), P(None, "st")),
        check_vma=False,
    )
```

```python
import math

import jax
import jax.numpy as jnp
from jax import lax
from jax.experimental import pallas as pl
from jax.experimental.layout import Layout, with_layout_constraint
from jax.experimental.pallas import tpu as pltpu
from jax.sharding import PartitionSpec as P

HIGHEST = lax.Precision.HIGHEST
BF16 = jnp.bfloat16
F32 = jnp.float32
CHUNKS = 4

VMEM = pl.BlockSpec(memory_space=pltpu.VMEM)
SMEM = pl.BlockSpec(memory_space=pltpu.SMEM)


def limit(mib):
    return pltpu.CompilerParams(vmem_limit_bytes=mib << 20)


def after(values, gate):
    return values if gate is None else lax.optimization_barrier((values, gate))[0]


def row_major(x):
    return with_layout_constraint(x, Layout(major_to_minor=tuple(range(x.ndim))))


def kernel_tile(emb_left, emb_right, amplitude):
    cross_term = lax.dot_general(emb_left, emb_right, (((0,), (0,)), ((), ())), precision=HIGHEST)
    norm_left = jnp.sum(emb_left * emb_left, axis=0)
    norm_right = jnp.sum(emb_right * emb_right, axis=0)
    distance = norm_left[:, None] + norm_right[None, :] - 2.0 * cross_term
    return jnp.exp(distance * (-0.5 / emb_left.shape[0])) * amplitude


def cyclic(x, axis, size, shift):
    return lax.ppermute(x, axis, [(i, (i + shift) % size) for i in range(size)])


def flip(x, axis, size, mask):
    return lax.ppermute(x, axis, [(i, i ^ mask) for i in range(size)])


def mix_hours(mixer, pieces):
    peers = len(pieces)
    chans, hours, rows = pieces[0].shape

    def body(mixer_ref, *refs):
        ins, outs = refs[:peers], refs[peers:]
        for c in range(chans):
            whole = jnp.concatenate([r[c] for r in ins], axis=0)
            mixed = jnp.dot(mixer_ref[...], whole, preferred_element_type=F32).astype(BF16)
            for e in range(peers):
                outs[e][c] = mixed[e * hours : (e + 1) * hours]

    return pl.pallas_call(
        body,
        out_shape=[jax.ShapeDtypeStruct((chans, hours, rows), BF16)] * peers,
        in_specs=[VMEM] * (1 + peers),
        out_specs=[VMEM] * peers,
        compiler_params=limit(4),
        name="mix_hours",
    )(mixer, *pieces)


def in_order(places, pieces):
    peers = len(pieces)
    chans, hours, rows = pieces[0].shape

    def body(places_ref, *refs):
        out = refs[peers]
        for e in range(peers):
            out[pl.ds(places_ref[e] * chans, chans)] = refs[e][...]

    return pl.pallas_call(
        body,
        out_shape=jax.ShapeDtypeStruct((peers * chans, hours, rows), BF16),
        in_specs=[SMEM] + [VMEM] * peers,
        out_specs=VMEM,
        compiler_params=limit(4),
        name="in_order",
    )(places, *pieces)


def joined(refs, shape):
    out, at = [], 0
    for count in shape:
        parts = [r[...] for r in refs[at : at + count]]
        out.append(parts[0] if count == 1 else jnp.concatenate(parts, axis=0))
        at += count
    return out


def apply_kernel(ker_bf, parts, shape):
    total = len(parts)
    length = sum(p.shape[0] for p in parts[: shape[0]])
    width = parts[0].shape[1]

    def body(ker_ref, *refs):
        blocks = joined(refs[:total], shape)
        acc = None
        for q, block in enumerate(blocks):
            term = jnp.dot(
                block, ker_ref[q * width : (q + 1) * width, :], preferred_element_type=F32
            )
            acc = term if acc is None else acc + term
        refs[total][...] = acc[:, :width]
        refs[total + 1][...] = acc[:, width:].astype(BF16)

    return pl.pallas_call(
        body,
        out_shape=[
            jax.ShapeDtypeStruct((length, width), F32),
            jax.ShapeDtypeStruct((length, width), BF16),
        ],
        in_specs=[VMEM] * (1 + total),
        out_specs=[VMEM] * 2,
        compiler_params=limit(8),
        name="apply_kernel",
    )(ker_bf, *parts)


def add_gram(gram, field_rows, parts, shape):
    total = len(parts)
    sides = len(field_rows)
    first = gram is None
    width = parts[0].shape[1]
    height = field_rows[0].shape[0]
    lead = 0 if first else 1

    def body(*refs):
        out = refs[-1]
        blocks = joined(refs[lead + sides : lead + sides + total], shape)
        for s in range(sides):
            left = refs[lead + s][...]
            for q, block in enumerate(blocks):
                term = jnp.dot(left, block, preferred_element_type=F32)
                at = (slice(s * height, (s + 1) * height), slice(q * width, (q + 1) * width))
                out[at] = term if first else refs[0][at] + term

    args = ([] if first else [gram]) + list(field_rows) + list(parts)
    return pl.pallas_call(
        body,
        out_shape=jax.ShapeDtypeStruct((sides * height, len(shape) * width), F32),
        in_specs=[VMEM] * len(args),
        out_specs=VMEM,
        input_output_aliases={} if first else {0: 0},
        compiler_params=limit(8),
        name="add_gram",
    )(*args)


def first_round(block, stations):
    bits = range((stations // 2 - 1).bit_length())
    return {0: [block]} | {1 << b: [flip(block, "st", stations, 2 << b)] for b in bits}


def other_rounds(parts_of, stations):
    chips = stations // 2
    rows = parts_of[0][0].shape[0]
    unit = 16
    parts_of = dict(parts_of)
    for q in sorted(range(1, chips), key=lambda v: (bin(v).count("1"), v)):
        if q in parts_of:
            continue
        bits = [b for b in range(q.bit_length()) if q >> b & 1]
        cuts = [rows // unit * a // len(bits) * unit for a in range(len(bits) + 1)]
        parts = []
        for a, b in enumerate(bits):
            source = parts_of[q ^ (1 << b)]
            source = source[0] if len(source) == 1 else jnp.concatenate(source, axis=0)
            parts.append(flip(source[cuts[a] : cuts[a + 1]], "st", stations, 2 << b))
        parts_of[q] = parts
    flat = [p for q in range(chips) for p in parts_of[q]]
    return flat, [len(parts_of[q]) for q in range(chips)]


def on_device(cotangent, field, temporal, embed):
    hours, chans, rows = cotangent.shape
    emb_width = embed.shape[0]
    stations = lax.axis_size("st")
    peers = lax.axis_size("hr")
    chips = stations // 2
    here = lax.axis_index("hr")
    amplitude = 1.0 / math.sqrt(rows * stations)
    group = chans // CHUNKS
    share = group // peers

    behind = [(here + peers - d) % peers for d in range(peers)]
    ahead = [(here + d) % peers for d in range(peers)]
    places = jnp.stack(behind).astype(jnp.int32)

    mixer = jnp.concatenate(
        [lax.dynamic_slice_in_dim(temporal, b * hours, hours, 0) for b in behind], axis=0
    )
    mixer = jnp.concatenate(
        [lax.dynamic_slice_in_dim(mixer, a * hours, hours, 1) for a in ahead], axis=1
    ).T

    def turned(k, gate):
        part = after(cotangent[:, k * group : (k + 1) * group], gate)
        part = row_major(jnp.transpose(part, (1, 0, 2)))
        return [lax.dynamic_slice_in_dim(part, a * share, share, 0) for a in ahead]

    def turned_field(k, gate):
        part = after(field[:, k * group : (k + 1) * group], gate)
        part = row_major(jnp.transpose(part, (2, 1, 0)).reshape(rows, group * hours))
        return [part, flip(part, "st", stations, 1)]

    def exchange(pieces):
        return [p if d == 0 else cyclic(p, "hr", peers, d) for d, p in enumerate(pieces)]

    pieces = [turned(0, None)]
    pieces.append(turned(1, pieces[0]))
    sent = {k: exchange(pieces[k]) for k in range(2)}

    embed = after(embed, pieces[1])
    emb_rows = jnp.concatenate([embed, flip(embed, "st", stations, 1)], axis=1)
    emb_cols = jnp.concatenate(
        [embed] + [flip(embed, "st", stations, 2 * q) for q in range(1, chips)], axis=1
    )
    pieces += [turned(k, emb_cols) for k in range(2, CHUNKS)]
    field_rows = [turned_field(k, pieces[-1]) for k in range(CHUNKS)]
    ker = kernel_tile(emb_rows, emb_cols, amplitude)
    ker_bf = ker.astype(BF16).T

    state = {"gate": None, "gram": None}
    blocks, outs = {}, {}

    def mix(k):
        mixed = mix_hours(mixer, after(sent[k], state["gate"]))
        state["gate"] = mixed
        back = exchange(mixed)
        if k + 2 < CHUNKS:
            sent[k + 2] = exchange(after(pieces[k + 2], mixed))
        blocks[k] = back

    def order(k):
        block = in_order(places, after(blocks[k], state["gate"])).reshape(group * hours, rows)
        state["gate"] = block
        blocks[k] = first_round(block, stations)

    def relay(k):
        blocks[k] = other_rounds(after(blocks[k], state["gate"]), stations)

    def contract(k):
        parts, shape = blocks[k]
        state["gram"] = add_gram(state["gram"], field_rows[k], parts, shape)
        ker_k, parts = after((ker_bf, parts), state["gram"])
        own, other = apply_kernel(ker_k, parts, shape)
        state["gate"] = own
        total = own + flip(other, "st", stations, 1).astype(F32)
        total = total.astype(BF16).reshape(group, hours, rows)
        outs[k] = jnp.transpose(total, (1, 0, 2))

    steps = []
    for k in range(CHUNKS):
        steps += [(mix, 2 * k + 0.5), (order, 2 * k + 3), (relay, 2 * k + 4.6), (contract, 2 * k + 4.8)]
    plan = sorted(((at, i // 4, step) for i, (step, at) in enumerate(steps)), key=lambda v: v[:2])
    for _, k, step in plan:
        step(k)
    field_grad = jnp.concatenate([outs[k] for k in range(CHUNKS)], axis=1)
    gram = state["gram"]

    weight = gram * ker
    by_row = lax.dot_general(emb_cols, weight, (((1,), (1,)), ((), ())), precision=HIGHEST)
    by_row = by_row - emb_rows * jnp.sum(weight, axis=1)[None, :]
    by_col = jnp.dot(emb_rows, weight, precision=HIGHEST)
    by_col = by_col - emb_cols * jnp.sum(weight, axis=0)[None, :]
    scale = 1.0 / emb_width
    by_row = by_row * scale
    by_col = by_col * scale
    part = by_row[:, :rows] + by_col[:, :rows] + flip(by_row[:, rows:], "st", stations, 1)
    for q in range(1, chips):
        part = part + flip(by_col[:, q * rows : (q + 1) * rows], "st", stations, 2 * q)
    embed_grad = part
    for d in range(1, peers):
        embed_grad = embed_grad + cyclic(part, "hr", peers, d)
    return (field_grad, embed_grad)


def solution(mesh):
    return jax.shard_map(
        on_device,
        mesh=mesh,
        in_specs=(P("hr", None, "st"), P("hr", None, "st"), P(), P(None, "st")),
        out_specs=(P("hr", None, "st"), P(None, "st")),
        check_vma=False,
    )
```

```python
import math

import jax
import jax.numpy as jnp
from jax import lax
from jax.experimental import pallas as pl
from jax.experimental.layout import Layout, with_layout_constraint
from jax.experimental.pallas import tpu as pltpu
from jax.sharding import PartitionSpec as P


HIGHEST = lax.Precision.HIGHEST
BF16 = jnp.bfloat16
F32 = jnp.float32
CHUNKS = 4

VMEM = pl.BlockSpec(memory_space=pltpu.VMEM)
SMEM = pl.BlockSpec(memory_space=pltpu.SMEM)


def limit(mib):
    return pltpu.CompilerParams(vmem_limit_bytes=mib << 20)


def after(values, gate):
    return values if gate is None else lax.optimization_barrier((values, gate))[0]


def row_major(x):
    return with_layout_constraint(x, Layout(major_to_minor=tuple(range(x.ndim))))


def kernel_tile(emb_left, emb_right, amplitude):
    cross_term = lax.dot_general(emb_left, emb_right, (((0,), (0,)), ((), ())), precision=HIGHEST)
    norm_left = jnp.sum(emb_left * emb_left, axis=0)
    norm_right = jnp.sum(emb_right * emb_right, axis=0)
    distance = norm_left[:, None] + norm_right[None, :] - 2.0 * cross_term
    return jnp.exp(distance * (-0.5 / emb_left.shape[0])) * amplitude


def cyclic(x, axis, size, shift):
    return lax.ppermute(x, axis, [(i, (i + shift) % size) for i in range(size)])


def flip(x, axis, size, mask):
    return lax.ppermute(x, axis, [(i, i ^ mask) for i in range(size)])


def mix_hours(mixer, pieces):
    peers = len(pieces)
    chans, hours, rows = pieces[0].shape

    def body(mixer_ref, *refs):
        ins, outs = refs[:peers], refs[peers:]
        for c in range(chans):
            whole = jnp.concatenate([r[c] for r in ins], axis=0)
            mixed = jnp.dot(mixer_ref[...], whole, preferred_element_type=F32).astype(BF16)
            for e in range(peers):
                outs[e][c] = mixed[e * hours : (e + 1) * hours]

    return pl.pallas_call(
        body,
        out_shape=[jax.ShapeDtypeStruct((chans, hours, rows), BF16)] * peers,
        in_specs=[VMEM] * (1 + peers),
        out_specs=[VMEM] * peers,
        compiler_params=limit(4),
        name="mix_hours",
    )(mixer, *pieces)


def in_order(places, pieces):
    peers = len(pieces)
    chans, hours, rows = pieces[0].shape

    def body(places_ref, *refs):
        out = refs[peers]
        for e in range(peers):
            out[pl.ds(places_ref[e] * chans, chans)] = refs[e][...]

    return pl.pallas_call(
        body,
        out_shape=jax.ShapeDtypeStruct((peers * chans, hours, rows), BF16),
        in_specs=[SMEM] + [VMEM] * peers,
        out_specs=VMEM,
        compiler_params=limit(4),
        name="in_order",
    )(places, *pieces)


def joined(refs, shape):
    out, at = [], 0
    for count in shape:
        parts = [r[...] for r in refs[at : at + count]]
        out.append(parts[0] if count == 1 else jnp.concatenate(parts, axis=0))
        at += count
    return out


def apply_kernel(ker_bf, parts, shape):
    total = len(parts)
    length = sum(p.shape[0] for p in parts[: shape[0]])
    width = parts[0].shape[1]

    def body(ker_ref, *refs):
        blocks = joined(refs[:total], shape)
        acc = None
        for q, block in enumerate(blocks):
            term = jnp.dot(
                block, ker_ref[q * width : (q + 1) * width, :], preferred_element_type=F32
            )
            acc = term if acc is None else acc + term
        refs[total][...] = acc[:, :width]
        refs[total + 1][...] = acc[:, width:].astype(BF16)

    return pl.pallas_call(
        body,
        out_shape=[
            jax.ShapeDtypeStruct((length, width), F32),
            jax.ShapeDtypeStruct((length, width), BF16),
        ],
        in_specs=[VMEM] * (1 + total),
        out_specs=[VMEM] * 2,
        compiler_params=limit(8),
        name="apply_kernel",
    )(ker_bf, *parts)


def add_gram(gram, field_rows, parts, shape):
    total = len(parts)
    sides = len(field_rows)
    first = gram is None
    width = parts[0].shape[1]
    height = field_rows[0].shape[0]
    lead = 0 if first else 1

    def body(*refs):
        out = refs[-1]
        blocks = joined(refs[lead + sides : lead + sides + total], shape)
        for s in range(sides):
            left = refs[lead + s][...]
            for q, block in enumerate(blocks):
                term = jnp.dot(left, block, preferred_element_type=F32)
                at = (slice(s * height, (s + 1) * height), slice(q * width, (q + 1) * width))
                out[at] = term if first else refs[0][at] + term

    args = ([] if first else [gram]) + list(field_rows) + list(parts)
    return pl.pallas_call(
        body,
        out_shape=jax.ShapeDtypeStruct((sides * height, len(shape) * width), F32),
        in_specs=[VMEM] * len(args),
        out_specs=VMEM,
        input_output_aliases={} if first else {0: 0},
        compiler_params=limit(8),
        name="add_gram",
    )(*args)


def exact_rows(emb):
    high = emb.astype(BF16)
    rest = emb - high.astype(F32)
    middle = rest.astype(BF16)
    low = (rest - middle.astype(F32)).astype(BF16)
    return jnp.concatenate([high, middle, low, jnp.ones(emb.shape, BF16)], axis=0)


def embed_parts(gram, ker, emb_rows, emb_cols, width):
    emb_width = emb_rows.shape[0]
    sides = emb_rows.shape[1] // width
    chips = emb_cols.shape[1] // width
    scale = 1.0 / emb_width

    def differences(sums, emb):
        total = sums[:emb_width] + sums[emb_width : 2 * emb_width]
        total = total + sums[2 * emb_width : 3 * emb_width]
        return (total - emb * sums[3 * emb_width : 3 * emb_width + 1]) * scale

    def body(gram_ref, ker_ref, rows_ref, cols_ref, *outs):
        weight = (gram_ref[...] * ker_ref[...]).astype(BF16)
        emb_r, emb_c = rows_ref[...], cols_ref[...]
        by_row = lax.dot_general(
            exact_rows(emb_c), weight, (((1,), (1,)), ((), ())), preferred_element_type=F32
        )
        by_row = differences(by_row, emb_r)
        by_col = jnp.dot(exact_rows(emb_r), weight, preferred_element_type=F32)
        by_col = differences(by_col, emb_c)
        outs[0][...] = by_row[:, :width] + by_col[:, :width]
        for s in range(1, sides):
            outs[s][...] = by_row[:, s * width : (s + 1) * width]
        for q in range(1, chips):
            outs[sides - 1 + q][...] = by_col[:, q * width : (q + 1) * width]

    count = sides + chips - 1
    return pl.pallas_call(
        body,
        out_shape=[jax.ShapeDtypeStruct((emb_width, width), F32)] * count,
        in_specs=[VMEM] * 4,
        out_specs=[VMEM] * count,
        compiler_params=limit(8),
        name="embed_parts",
    )(gram, ker, emb_rows, emb_cols)


def first_round(block, stations):
    bits = range((stations // 2 - 1).bit_length())
    return {0: [block]} | {1 << b: [flip(block, "st", stations, 2 << b)] for b in bits}


def other_rounds(parts_of, stations):
    chips = stations // 2
    rows = parts_of[0][0].shape[0]
    unit = 16
    parts_of = dict(parts_of)
    for q in sorted(range(1, chips), key=lambda v: (bin(v).count("1"), v)):
        if q in parts_of:
            continue
        bits = [b for b in range(q.bit_length()) if q >> b & 1]
        cuts = [rows // unit * a // len(bits) * unit for a in range(len(bits) + 1)]
        parts = []
        for a, b in enumerate(bits):
            source = parts_of[q ^ (1 << b)]
            source = source[0] if len(source) == 1 else jnp.concatenate(source, axis=0)
            parts.append(flip(source[cuts[a] : cuts[a + 1]], "st", stations, 2 << b))
        parts_of[q] = parts
    flat = [p for q in range(chips) for p in parts_of[q]]
    return flat, [len(parts_of[q]) for q in range(chips)]


def on_device(cotangent, field, temporal, embed):
    hours, chans, rows = cotangent.shape
    stations = lax.axis_size("st")
    peers = lax.axis_size("hr")
    chips = stations // 2
    here = lax.axis_index("hr")
    amplitude = 1.0 / math.sqrt(rows * stations)
    group = chans // CHUNKS
    share = group // peers

    behind = [(here + peers - d) % peers for d in range(peers)]
    ahead = [(here + d) % peers for d in range(peers)]
    places = jnp.stack(behind).astype(jnp.int32)

    mixer = jnp.concatenate(
        [lax.dynamic_slice_in_dim(temporal, b * hours, hours, 0) for b in behind], axis=0
    )
    mixer = jnp.concatenate(
        [lax.dynamic_slice_in_dim(mixer, a * hours, hours, 1) for a in ahead], axis=1
    ).T

    def turned(k, gate):
        part = after(cotangent[:, k * group : (k + 1) * group], gate)
        part = row_major(jnp.transpose(part, (1, 0, 2)))
        return [lax.dynamic_slice_in_dim(part, a * share, share, 0) for a in ahead]

    def turned_field(k, gate):
        part = after(field[:, k * group : (k + 1) * group], gate)
        part = row_major(jnp.transpose(part, (2, 1, 0)).reshape(rows, group * hours))
        return [part, flip(part, "st", stations, 1)]

    def exchange(pieces):
        return [p if d == 0 else cyclic(p, "hr", peers, d) for d, p in enumerate(pieces)]

    pieces = [turned(0, None)]
    pieces.append(turned(1, pieces[0]))
    sent = {k: exchange(pieces[k]) for k in range(2)}

    embed = after(embed, pieces[1])
    emb_rows = jnp.concatenate([embed, flip(embed, "st", stations, 1)], axis=1)
    emb_cols = jnp.concatenate(
        [embed] + [flip(embed, "st", stations, 2 * q) for q in range(1, chips)], axis=1
    )
    pieces += [turned(k, emb_cols) for k in range(2, CHUNKS)]
    field_rows = [turned_field(k, pieces[-1]) for k in range(CHUNKS)]
    ker = kernel_tile(emb_rows, emb_cols, amplitude)
    ker_bf = ker.astype(BF16).T

    state = {"gate": None, "gram": None}
    blocks, outs = {}, {}

    def mix(k):
        inputs = after(sent[k], state["gate"])
        mixed = mix_hours(mixer, inputs)
        state["gate"] = mixed
        blocks[k] = exchange(mixed)
        if k + 2 < CHUNKS:
            sent[k + 2] = exchange(after(pieces[k + 2], mixed))

    def order(k):
        gate = state["gate"] if k else (state["gate"], ker, ker_bf, field_rows)
        inputs = after(blocks[k], gate)
        block = in_order(places, inputs).reshape(group * hours, rows)
        state["gate"] = block
        blocks[k] = first_round(block, stations)

    def relay(k):
        inputs = after(blocks[k], state["gate"])
        blocks[k] = other_rounds(inputs, stations)

    def contract(k):
        parts, shape = blocks[k]
        state["gram"] = add_gram(state["gram"], field_rows[k], parts, shape)
        ker_k, parts = after((ker_bf, parts), state["gram"])
        own, other = apply_kernel(ker_k, parts, shape)
        state["gate"] = own
        other = flip(other, "st", stations, 1)
        total = (own + other.astype(F32)).astype(BF16).reshape(group, hours, rows)
        outs[k] = jnp.transpose(total, (1, 0, 2))

    run = {"mix": mix, "order": order, "relay": relay, "contract": contract}
    for name, k in plan():
        run[name](k)
    field_grad = jnp.concatenate([outs[k] for k in range(CHUNKS)], axis=1)

    parts = embed_parts(state["gram"], ker, emb_rows, emb_cols, rows)
    part = parts[0] + flip(parts[1], "st", stations, 1)
    for q in range(1, chips):
        part = part + flip(parts[1 + q], "st", stations, 2 * q)
    embed_grad = part
    for d in range(1, peers):
        embed_grad = embed_grad + cyclic(part, "hr", peers, d)
    return (field_grad, embed_grad)


def plan():
    at = {"mix": 0.5, "order": 3.0, "relay": 4.6, "contract": 4.8}
    steps = [(2 * k + t, k, name) for k in range(CHUNKS) for name, t in at.items()]
    return [(name, k) for _, k, name in sorted(steps)]


def solution(mesh):
    return jax.shard_map(
        on_device,
        mesh=mesh,
        in_specs=(P("hr", None, "st"), P("hr", None, "st"), P(), P(None, "st")),
        out_specs=(P("hr", None, "st"), P(None, "st")),
        check_vma=False,
    )
```

```python
import math

import jax
import jax.numpy as jnp
from jax import lax
from jax.experimental import pallas as pl
from jax.experimental.layout import Layout, with_layout_constraint
from jax.experimental.pallas import tpu as pltpu
from jax.sharding import PartitionSpec as P


HIGHEST = lax.Precision.HIGHEST
BF16 = jnp.bfloat16
F32 = jnp.float32
CHUNKS = 4

VMEM = pl.BlockSpec(memory_space=pltpu.VMEM)
SMEM = pl.BlockSpec(memory_space=pltpu.SMEM)


def limit(mib):
    return pltpu.CompilerParams(vmem_limit_bytes=mib << 20)


def after(values, gate):
    return values if gate is None else lax.optimization_barrier((values, gate))[0]


def row_major(x):
    return with_layout_constraint(x, Layout(major_to_minor=tuple(range(x.ndim))))


def kernel_matrix(left, right, amplitude):
    emb_width, width = left[0].shape
    n_left, n_right = len(left), len(right)

    def body(*refs):
        rows = jnp.concatenate([r[...] for r in refs[:n_left]], axis=1)
        cols = jnp.concatenate([r[...] for r in refs[n_left : n_left + n_right]], axis=1)
        ker, ker_bf, rows_out, cols_out = refs[n_left + n_right :]
        rows_out[...] = rows
        cols_out[...] = cols
        rows_t = rows.T
        norm_rows = jnp.sum(rows_t * rows_t, axis=1, keepdims=True)
        norm_cols = jnp.sum(cols * cols, axis=0, keepdims=True)
        cross = jnp.dot(rows_t, cols, precision=HIGHEST, preferred_element_type=F32)
        distance = norm_rows + norm_cols - 2.0 * cross
        tile = jnp.exp(distance * (-0.5 / emb_width)) * amplitude
        ker[...] = tile
        ker_bf[...] = tile.astype(BF16)

    shape = (n_left * width, n_right * width)
    return pl.pallas_call(
        body,
        out_shape=[
            jax.ShapeDtypeStruct(shape, F32),
            jax.ShapeDtypeStruct(shape, BF16),
            jax.ShapeDtypeStruct((emb_width, shape[0]), F32),
            jax.ShapeDtypeStruct((emb_width, shape[1]), F32),
        ],
        in_specs=[VMEM] * (n_left + n_right),
        out_specs=[VMEM] * 4,
        compiler_params=limit(12),
        name="kernel_matrix",
    )(*left, *right)


def cyclic(x, axis, size, shift):
    return lax.ppermute(x, axis, [(i, (i + shift) % size) for i in range(size)])


def flip(x, axis, size, mask):
    return lax.ppermute(x, axis, [(i, i ^ mask) for i in range(size)])


def mix_hours(mixer, pieces):
    peers = len(pieces)
    chans, hours, rows = pieces[0].shape

    def body(mixer_ref, *refs):
        ins, outs = refs[:peers], refs[peers:]
        for c in range(chans):
            whole = jnp.concatenate([r[c] for r in ins], axis=0)
            mixed = jnp.dot(mixer_ref[...], whole, preferred_element_type=F32).astype(BF16)
            for e in range(peers):
                outs[e][c] = mixed[e * hours : (e + 1) * hours]

    return pl.pallas_call(
        body,
        out_shape=[jax.ShapeDtypeStruct((chans, hours, rows), BF16)] * peers,
        in_specs=[VMEM] * (1 + peers),
        out_specs=[VMEM] * peers,
        compiler_params=limit(4),
        name="mix_hours",
    )(mixer, *pieces)


def in_order(places, pieces):
    peers = len(pieces)
    chans, hours, rows = pieces[0].shape

    def body(places_ref, *refs):
        out = refs[peers]
        for e in range(peers):
            out[pl.ds(places_ref[e] * chans, chans)] = refs[e][...]

    return pl.pallas_call(
        body,
        out_shape=jax.ShapeDtypeStruct((peers * chans, hours, rows), BF16),
        in_specs=[SMEM] + [VMEM] * peers,
        out_specs=VMEM,
        compiler_params=limit(4),
        name="in_order",
    )(places, *pieces)


def joined(refs, shape):
    out, at = [], 0
    for count in shape:
        parts = [r[...] for r in refs[at : at + count]]
        out.append(parts[0] if count == 1 else jnp.concatenate(parts, axis=0))
        at += count
    return out


def apply_kernel(ker_bf, parts, shape):
    total = len(parts)
    length = sum(p.shape[0] for p in parts[: shape[0]])
    width = parts[0].shape[1]

    def body(ker_ref, *refs):
        blocks = joined(refs[:total], shape)
        acc = None
        for q, block in enumerate(blocks):
            term = lax.dot_general(
                block,
                ker_ref[:, q * width : (q + 1) * width],
                (((1,), (1,)), ((), ())),
                preferred_element_type=F32,
            )
            acc = term if acc is None else acc + term
        refs[total][...] = acc[:, :width]
        refs[total + 1][...] = acc[:, width:].astype(BF16)

    return pl.pallas_call(
        body,
        out_shape=[
            jax.ShapeDtypeStruct((length, width), F32),
            jax.ShapeDtypeStruct((length, width), BF16),
        ],
        in_specs=[VMEM] * (1 + total),
        out_specs=[VMEM] * 2,
        compiler_params=limit(8),
        name="apply_kernel",
    )(ker_bf, *parts)


def add_gram(gram, field_rows, parts, shape):
    total = len(parts)
    sides = len(field_rows)
    first = gram is None
    width = parts[0].shape[1]
    height = field_rows[0].shape[0]
    lead = 0 if first else 1

    def body(*refs):
        out = refs[-1]
        blocks = joined(refs[lead + sides : lead + sides + total], shape)
        for s in range(sides):
            left = refs[lead + s][...]
            for q, block in enumerate(blocks):
                term = jnp.dot(left, block, preferred_element_type=F32)
                at = (slice(s * height, (s + 1) * height), slice(q * width, (q + 1) * width))
                out[at] = term if first else refs[0][at] + term

    args = ([] if first else [gram]) + list(field_rows) + list(parts)
    return pl.pallas_call(
        body,
        out_shape=jax.ShapeDtypeStruct((sides * height, len(shape) * width), F32),
        in_specs=[VMEM] * len(args),
        out_specs=VMEM,
        input_output_aliases={} if first else {0: 0},
        compiler_params=limit(8),
        name="add_gram",
    )(*args)


def exact_rows(emb):
    high = emb.astype(BF16)
    rest = emb - high.astype(F32)
    middle = rest.astype(BF16)
    low = (rest - middle.astype(F32)).astype(BF16)
    return jnp.concatenate([high, middle, low, jnp.ones(emb.shape, BF16)], axis=0)


def embed_parts(gram, ker, emb_rows, emb_cols, width):
    emb_width = emb_rows.shape[0]
    sides = emb_rows.shape[1] // width
    chips = emb_cols.shape[1] // width
    scale = 1.0 / emb_width

    def differences(sums, emb):
        total = sums[:emb_width] + sums[emb_width : 2 * emb_width]
        total = total + sums[2 * emb_width : 3 * emb_width]
        return (total - emb * sums[3 * emb_width : 3 * emb_width + 1]) * scale

    def body(gram_ref, ker_ref, rows_ref, cols_ref, *outs):
        weight = (gram_ref[...] * ker_ref[...]).astype(BF16)
        emb_r, emb_c = rows_ref[...], cols_ref[...]
        by_row = lax.dot_general(
            exact_rows(emb_c), weight, (((1,), (1,)), ((), ())), preferred_element_type=F32
        )
        by_row = differences(by_row, emb_r)
        by_col = jnp.dot(exact_rows(emb_r), weight, preferred_element_type=F32)
        by_col = differences(by_col, emb_c)
        outs[0][...] = by_row[:, :width] + by_col[:, :width]
        for s in range(1, sides):
            outs[s][...] = by_row[:, s * width : (s + 1) * width]
        for q in range(1, chips):
            outs[sides - 1 + q][...] = by_col[:, q * width : (q + 1) * width]

    count = sides + chips - 1
    return pl.pallas_call(
        body,
        out_shape=[jax.ShapeDtypeStruct((emb_width, width), F32)] * count,
        in_specs=[VMEM] * 4,
        out_specs=[VMEM] * count,
        compiler_params=limit(8),
        name="embed_parts",
    )(gram, ker, emb_rows, emb_cols)


def first_round(block, stations):
    bits = range((stations // 2 - 1).bit_length())
    return {0: [block]} | {1 << b: [flip(block, "st", stations, 2 << b)] for b in bits}


def other_rounds(parts_of, stations):
    chips = stations // 2
    rows = parts_of[0][0].shape[0]
    unit = 16
    parts_of = dict(parts_of)
    for q in sorted(range(1, chips), key=lambda v: (bin(v).count("1"), v)):
        if q in parts_of:
            continue
        bits = [b for b in range(q.bit_length()) if q >> b & 1]
        cuts = [rows // unit * a // len(bits) * unit for a in range(len(bits) + 1)]
        parts = []
        for a, b in enumerate(bits):
            source = parts_of[q ^ (1 << b)]
            source = source[0] if len(source) == 1 else jnp.concatenate(source, axis=0)
            parts.append(flip(source[cuts[a] : cuts[a + 1]], "st", stations, 2 << b))
        parts_of[q] = parts
    flat = [p for q in range(chips) for p in parts_of[q]]
    return flat, [len(parts_of[q]) for q in range(chips)]


def on_device(cotangent, field, temporal, embed):
    hours, chans, rows = cotangent.shape
    stations = lax.axis_size("st")
    peers = lax.axis_size("hr")
    chips = stations // 2
    here = lax.axis_index("hr")
    amplitude = 1.0 / math.sqrt(rows * stations)
    group = chans // CHUNKS
    share = group // peers

    behind = [(here + peers - d) % peers for d in range(peers)]
    ahead = [(here + d) % peers for d in range(peers)]
    places = jnp.stack(behind).astype(jnp.int32)

    mixer = jnp.concatenate(
        [lax.dynamic_slice_in_dim(temporal, b * hours, hours, 0) for b in behind], axis=0
    )
    mixer = jnp.concatenate(
        [lax.dynamic_slice_in_dim(mixer, a * hours, hours, 1) for a in ahead], axis=1
    ).T

    def turned(source, k):
        part = source[:, k * group : (k + 1) * group]
        part = row_major(jnp.transpose(part, (1, 0, 2)))
        return [lax.dynamic_slice_in_dim(part, a * share, share, 0) for a in ahead]

    def exchange(pieces):
        return [p if d == 0 else cyclic(p, "hr", peers, d) for d, p in enumerate(pieces)]

    pieces = [turned(cotangent, 0)]
    rest = after(cotangent, pieces[0])
    pieces += [turned(rest, k) for k in range(1, CHUNKS)]
    sent = {k: exchange(pieces[k]) for k in range(CHUNKS)}

    own = after(embed, pieces[1])
    left = [own, flip(own, "st", stations, 1)]
    right = [own] + [flip(own, "st", stations, 2 * q) for q in range(1, chips)]
    ker, ker_bf, emb_rows, emb_cols = kernel_matrix(left, right, amplitude)

    def turned_field(source, k):
        part = source[:, k * group : (k + 1) * group]
        part = row_major(jnp.transpose(part, (2, 1, 0)).reshape(rows, group * hours))
        return [part, flip(part, "st", stations, 1)]

    source = after(field, right[1:])
    field_rows = [turned_field(source, k) for k in range(CHUNKS)]

    state = {"gram": None}
    blocks, outs = {}, {}

    def mix(k):
        mixed = mix_hours(mixer, sent[k])
        blocks[k] = exchange(mixed)

    def order(k):
        block = in_order(places, blocks[k]).reshape(group * hours, rows)
        blocks[k] = first_round(block, stations)

    def relay(k):
        blocks[k] = other_rounds(blocks[k], stations)

    def contract(k):
        parts, shape = blocks[k]
        state["gram"] = add_gram(state["gram"], field_rows[k], parts, shape)
        own, other = apply_kernel(ker_bf, parts, shape)
        other = flip(other, "st", stations, 1)
        total = (own + other.astype(F32)).astype(BF16).reshape(group, hours, rows)
        outs[k] = jnp.transpose(total, (1, 0, 2))

    run = {"mix": mix, "order": order, "relay": relay, "contract": contract}
    for name, k in plan():
        run[name](k)
    field_grad = jnp.concatenate([outs[k] for k in range(CHUNKS)], axis=1)

    parts = embed_parts(state["gram"], ker, emb_rows, emb_cols, rows)
    part = parts[0] + flip(parts[1], "st", stations, 1)
    for q in range(1, chips):
        part = part + flip(parts[1 + q], "st", stations, 2 * q)
    embed_grad = part
    for d in range(1, peers):
        embed_grad = embed_grad + cyclic(part, "hr", peers, d)
    return (field_grad, embed_grad)


def plan():
    at = {"mix": 0.5, "order": 3.0, "relay": 4.6, "contract": 5.2}
    steps = [(2 * k + t, k, name) for k in range(CHUNKS) for name, t in at.items()]
    return [(name, k) for _, k, name in sorted(steps)]


def solution(mesh):
    return jax.shard_map(
        on_device,
        mesh=mesh,
        in_specs=(P("hr", None, "st"), P("hr", None, "st"), P(), P(None, "st")),
        out_specs=(P("hr", None, "st"), P(None, "st")),
        check_vma=False,
    )
```

```python
import math

import jax
import jax.numpy as jnp
from jax import lax
from jax.experimental import pallas as pl
from jax.experimental.layout import Layout, with_layout_constraint
from jax.experimental.pallas import tpu as pltpu
from jax.sharding import PartitionSpec as P


HIGHEST = lax.Precision.HIGHEST
BF16 = jnp.bfloat16
F32 = jnp.float32
CHUNKS = 4

VMEM = pl.BlockSpec(memory_space=pltpu.VMEM)
SMEM = pl.BlockSpec(memory_space=pltpu.SMEM)


def limit(mib):
    return pltpu.CompilerParams(vmem_limit_bytes=mib << 20)


def after(values, gate):
    return values if gate is None else lax.optimization_barrier((values, gate))[0]


def row_major(x):
    return with_layout_constraint(x, Layout(major_to_minor=tuple(range(x.ndim))))


def kernel_matrix(left, right, amplitude):
    emb_width, width = left[0].shape
    n_left, n_right = len(left), len(right)

    def body(*refs):
        rows = jnp.concatenate([r[...] for r in refs[:n_left]], axis=1)
        cols = jnp.concatenate([r[...] for r in refs[n_left : n_left + n_right]], axis=1)
        ker, ker_bf, rows_out, cols_out = refs[n_left + n_right :]
        rows_out[...] = rows
        cols_out[...] = cols
        rows_t = rows.T
        norm_rows = jnp.sum(rows_t * rows_t, axis=1, keepdims=True)
        norm_cols = jnp.sum(cols * cols, axis=0, keepdims=True)
        cross = jnp.dot(rows_t, cols, precision=HIGHEST, preferred_element_type=F32)
        distance = norm_rows + norm_cols - 2.0 * cross
        tile = jnp.exp(distance * (-0.5 / emb_width)) * amplitude
        ker[...] = tile
        ker_bf[...] = tile.astype(BF16)

    shape = (n_left * width, n_right * width)
    return pl.pallas_call(
        body,
        out_shape=[
            jax.ShapeDtypeStruct(shape, F32),
            jax.ShapeDtypeStruct(shape, BF16),
            jax.ShapeDtypeStruct((emb_width, shape[0]), F32),
            jax.ShapeDtypeStruct((emb_width, shape[1]), F32),
        ],
        in_specs=[VMEM] * (n_left + n_right),
        out_specs=[VMEM] * 4,
        compiler_params=limit(12),
        name="kernel_matrix",
    )(*left, *right)


def flip(x, axis, size, mask):
    return lax.ppermute(x, axis, [(i, i ^ mask) for i in range(size)])


def mix_hours(mixer, pieces):
    peers = len(pieces)
    chans, hours, rows = pieces[0].shape

    def body(mixer_ref, *refs):
        ins, outs = refs[:peers], refs[peers:]
        for c in range(chans):
            whole = jnp.concatenate([r[c] for r in ins], axis=0)
            mixed = jnp.dot(mixer_ref[...], whole, preferred_element_type=F32).astype(BF16)
            for e in range(peers):
                outs[e][c] = mixed[e * hours : (e + 1) * hours]

    return pl.pallas_call(
        body,
        out_shape=[jax.ShapeDtypeStruct((chans, hours, rows), BF16)] * peers,
        in_specs=[VMEM] * (1 + peers),
        out_specs=[VMEM] * peers,
        compiler_params=limit(4),
        name="mix_hours",
    )(mixer, *pieces)


def in_order(places, pieces):
    peers = len(pieces)
    chans, hours, rows = pieces[0].shape

    def body(places_ref, *refs):
        out = refs[peers]
        for e in range(peers):
            out[pl.ds(places_ref[e] * chans, chans)] = refs[e][...]

    return pl.pallas_call(
        body,
        out_shape=jax.ShapeDtypeStruct((peers * chans, hours, rows), BF16),
        in_specs=[SMEM] + [VMEM] * peers,
        out_specs=VMEM,
        compiler_params=limit(4),
        name="in_order",
    )(places, *pieces)


def joined(refs, shape):
    out, at = [], 0
    for count in shape:
        parts = [r[...] for r in refs[at : at + count]]
        out.append(parts[0] if count == 1 else jnp.concatenate(parts, axis=0))
        at += count
    return out


def apply_kernel(ker_bf, parts, shape):
    total = len(parts)
    length = sum(p.shape[0] for p in parts[: shape[0]])
    width = parts[0].shape[1]

    def body(ker_ref, *refs):
        blocks = joined(refs[:total], shape)
        acc = None
        for q, block in enumerate(blocks):
            term = lax.dot_general(
                block,
                ker_ref[:, q * width : (q + 1) * width],
                (((1,), (1,)), ((), ())),
                preferred_element_type=F32,
            )
            acc = term if acc is None else acc + term
        refs[total][...] = acc[:, :width]
        refs[total + 1][...] = acc[:, width:].astype(BF16)

    return pl.pallas_call(
        body,
        out_shape=[
            jax.ShapeDtypeStruct((length, width), F32),
            jax.ShapeDtypeStruct((length, width), BF16),
        ],
        in_specs=[VMEM] * (1 + total),
        out_specs=[VMEM] * 2,
        compiler_params=limit(8),
        name="apply_kernel",
    )(ker_bf, *parts)


def add_gram(gram, field_rows, parts, shape):
    total = len(parts)
    sides = len(field_rows)
    first = gram is None
    width = parts[0].shape[1]
    height = field_rows[0].shape[0]
    lead = 0 if first else 1

    def body(*refs):
        out = refs[-1]
        blocks = joined(refs[lead + sides : lead + sides + total], shape)
        for s in range(sides):
            left = refs[lead + s][...]
            for q, block in enumerate(blocks):
                term = jnp.dot(left, block, preferred_element_type=F32)
                at = (slice(s * height, (s + 1) * height), slice(q * width, (q + 1) * width))
                out[at] = term if first else refs[0][at] + term

    args = ([] if first else [gram]) + list(field_rows) + list(parts)
    return pl.pallas_call(
        body,
        out_shape=jax.ShapeDtypeStruct((sides * height, len(shape) * width), F32),
        in_specs=[VMEM] * len(args),
        out_specs=VMEM,
        input_output_aliases={} if first else {0: 0},
        compiler_params=limit(8),
        name="add_gram",
    )(*args)


def exact_rows(emb):
    high = emb.astype(BF16)
    rest = emb - high.astype(F32)
    middle = rest.astype(BF16)
    low = (rest - middle.astype(F32)).astype(BF16)
    return jnp.concatenate([high, middle, low, jnp.ones(emb.shape, BF16)], axis=0)


def embed_parts(gram, ker, emb_rows, emb_cols, width):
    emb_width = emb_rows.shape[0]
    sides = emb_rows.shape[1] // width
    chips = emb_cols.shape[1] // width
    scale = 1.0 / emb_width

    def differences(sums, emb):
        total = sums[:emb_width] + sums[emb_width : 2 * emb_width]
        total = total + sums[2 * emb_width : 3 * emb_width]
        return (total - emb * sums[3 * emb_width : 3 * emb_width + 1]) * scale

    def body(gram_ref, ker_ref, rows_ref, cols_ref, *outs):
        weight = (gram_ref[...] * ker_ref[...]).astype(BF16)
        emb_r, emb_c = rows_ref[...], cols_ref[...]
        by_row = lax.dot_general(
            exact_rows(emb_c), weight, (((1,), (1,)), ((), ())), preferred_element_type=F32
        )
        by_row = differences(by_row, emb_r)
        by_col = jnp.dot(exact_rows(emb_r), weight, preferred_element_type=F32)
        by_col = differences(by_col, emb_c)
        outs[0][...] = by_row[:, :width] + by_col[:, :width]
        for s in range(1, sides):
            outs[s][...] = by_row[:, s * width : (s + 1) * width]
        for q in range(1, chips):
            outs[sides - 1 + q][...] = by_col[:, q * width : (q + 1) * width]

    count = sides + chips - 1
    return pl.pallas_call(
        body,
        out_shape=[jax.ShapeDtypeStruct((emb_width, width), F32)] * count,
        in_specs=[VMEM] * 4,
        out_specs=[VMEM] * count,
        compiler_params=limit(8),
        name="embed_parts",
    )(gram, ker, emb_rows, emb_cols)


def first_round(block, stations):
    bits = range((stations // 2 - 1).bit_length())
    return {0: [block]} | {1 << b: [flip(block, "st", stations, 2 << b)] for b in bits}


def other_rounds(parts_of, stations):
    chips = stations // 2
    rows = parts_of[0][0].shape[0]
    unit = 16
    parts_of = dict(parts_of)
    for q in sorted(range(1, chips), key=lambda v: (bin(v).count("1"), v)):
        if q in parts_of:
            continue
        bits = [b for b in range(q.bit_length()) if q >> b & 1]
        cuts = [rows // unit * a // len(bits) * unit for a in range(len(bits) + 1)]
        parts = []
        for a, b in enumerate(bits):
            source = parts_of[q ^ (1 << b)]
            source = source[0] if len(source) == 1 else jnp.concatenate(source, axis=0)
            parts.append(flip(source[cuts[a] : cuts[a + 1]], "st", stations, 2 << b))
        parts_of[q] = parts
    flat = [p for q in range(chips) for p in parts_of[q]]
    return flat, [len(parts_of[q]) for q in range(chips)]


def on_device(cotangent, field, temporal, embed):
    hours, chans, rows = cotangent.shape
    stations = lax.axis_size("st")
    peers = lax.axis_size("hr")
    chips = stations // 2
    here = lax.axis_index("hr")
    amplitude = 1.0 / math.sqrt(rows * stations)
    group = chans // CHUNKS
    share = group // peers

    across = [here ^ d for d in range(peers)]
    places = jnp.stack(across).astype(jnp.int32)

    mixer = jnp.concatenate(
        [lax.dynamic_slice_in_dim(temporal, b * hours, hours, 0) for b in across], axis=0
    )
    mixer = jnp.concatenate(
        [lax.dynamic_slice_in_dim(mixer, a * hours, hours, 1) for a in across], axis=1
    ).T

    def turned(source, k):
        part = source[:, k * group : (k + 1) * group]
        part = row_major(jnp.transpose(part, (1, 0, 2)))
        return [lax.dynamic_slice_in_dim(part, a * share, share, 0) for a in across]

    def exchange(pieces):
        return [p if d == 0 else flip(p, "hr", peers, d) for d, p in enumerate(pieces)]

    pieces = [turned(cotangent, 0)]
    rest = after(cotangent, pieces[0])
    pieces += [turned(rest, k) for k in range(1, CHUNKS)]
    sent = {k: exchange(pieces[k]) for k in range(CHUNKS)}

    own = after(embed, pieces[1])
    left = [own, flip(own, "st", stations, 1)]
    right = [own] + [flip(own, "st", stations, 2 * q) for q in range(1, chips)]
    ker, ker_bf, emb_rows, emb_cols = kernel_matrix(left, right, amplitude)

    def turned_field(source, k):
        part = source[:, k * group : (k + 1) * group]
        part = row_major(jnp.transpose(part, (2, 1, 0)).reshape(rows, group * hours))
        return [part, flip(part, "st", stations, 1)]

    source = after(field, right[1:])
    field_rows = [turned_field(source, k) for k in range(CHUNKS)]

    state = {"gram": None}
    blocks, outs = {}, {}

    def mix(k):
        mixed = mix_hours(mixer, sent[k])
        blocks[k] = exchange(mixed)

    def order(k):
        block = in_order(places, blocks[k]).reshape(group * hours, rows)
        blocks[k] = first_round(block, stations)

    def relay(k):
        blocks[k] = other_rounds(blocks[k], stations)

    def contract(k):
        parts, shape = blocks[k]
        state["gram"] = add_gram(state["gram"], field_rows[k], parts, shape)
        own, other = apply_kernel(ker_bf, parts, shape)
        other = flip(other, "st", stations, 1)
        total = (own + other.astype(F32)).astype(BF16).reshape(group, hours, rows)
        outs[k] = jnp.transpose(total, (1, 0, 2))

    run = {"mix": mix, "order": order, "relay": relay, "contract": contract}
    for name, k in plan():
        run[name](k)
    field_grad = jnp.zeros(field.shape, BF16)
    for k in range(CHUNKS):
        field_grad = lax.dynamic_update_slice_in_dim(field_grad, outs[k], k * group, 1)

    parts = embed_parts(state["gram"], ker, emb_rows, emb_cols, rows)
    part = parts[0] + flip(parts[1], "st", stations, 1)
    for q in range(1, chips):
        part = part + flip(parts[1 + q], "st", stations, 2 * q)
    embed_grad = part
    for d in range(1, peers):
        embed_grad = embed_grad + flip(part, "hr", peers, d)
    return (field_grad, embed_grad)


def plan():
    at = {"mix": 0.5, "order": 3.0, "relay": 4.6, "contract": 5.2}
    steps = [(2 * k + t, k, name) for k in range(CHUNKS) for name, t in at.items()]
    return [(name, k) for _, k, name in sorted(steps)]


def solution(mesh):
    return jax.shard_map(
        on_device,
        mesh=mesh,
        in_specs=(P("hr", None, "st"), P("hr", None, "st"), P(), P(None, "st")),
        out_specs=(P("hr", None, "st"), P(None, "st")),
        check_vma=False,
    )
```

```python
import math

import jax
import jax.numpy as jnp
from jax import lax
from jax.experimental import pallas as pl
from jax.experimental.layout import Layout, with_layout_constraint
from jax.experimental.pallas import tpu as pltpu
from jax.sharding import PartitionSpec as P


HIGHEST = lax.Precision.HIGHEST
BF16 = jnp.bfloat16
F32 = jnp.float32
SPLIT = (3, 2, 2, 1)
CHUNKS = len(SPLIT)
PLAN = (
    "mix0 mix1 order0",
    "order1 relay0 mix2",
    "relay1 order2 contract0",
    "mix3 contract1 order3",
    "relay2 relay3 contract2",
    "contract3",
)

VMEM = pl.BlockSpec(memory_space=pltpu.VMEM)
SMEM = pl.BlockSpec(memory_space=pltpu.SMEM)


def limit(mib):
    return pltpu.CompilerParams(vmem_limit_bytes=mib << 20)


def after(values, gate):
    return values if gate is None else lax.optimization_barrier((values, gate))[0]


def row_major(x):
    return with_layout_constraint(x, Layout(major_to_minor=tuple(range(x.ndim))))


def kernel_matrix(left, right, amplitude):
    emb_width, width = left[0].shape
    n_left, n_right = len(left), len(right)

    def body(*refs):
        rows = jnp.concatenate([r[...] for r in refs[:n_left]], axis=1)
        cols = jnp.concatenate([r[...] for r in refs[n_left : n_left + n_right]], axis=1)
        ker, ker_bf, rows_out, cols_out = refs[n_left + n_right :]
        rows_out[...] = rows
        cols_out[...] = cols
        rows_t = rows.T
        norm_rows = jnp.sum(rows_t * rows_t, axis=1, keepdims=True)
        norm_cols = jnp.sum(cols * cols, axis=0, keepdims=True)
        cross = jnp.dot(rows_t, cols, precision=HIGHEST, preferred_element_type=F32)
        distance = norm_rows + norm_cols - 2.0 * cross
        tile = jnp.exp(distance * (-0.5 / emb_width)) * amplitude
        ker[...] = tile
        ker_bf[...] = tile.astype(BF16)

    shape = (n_left * width, n_right * width)
    return pl.pallas_call(
        body,
        out_shape=[
            jax.ShapeDtypeStruct(shape, F32),
            jax.ShapeDtypeStruct(shape, BF16),
            jax.ShapeDtypeStruct((emb_width, shape[0]), F32),
            jax.ShapeDtypeStruct((emb_width, shape[1]), F32),
        ],
        in_specs=[VMEM] * (n_left + n_right),
        out_specs=[VMEM] * 4,
        compiler_params=limit(12),
        name="kernel_matrix",
    )(*left, *right)


def flip(x, axis, size, mask):
    return lax.ppermute(x, axis, [(i, i ^ mask) for i in range(size)])


def mix_hours(mixer, pieces):
    peers = len(pieces)
    chans, hours, rows = pieces[0].shape

    def body(mixer_ref, *refs):
        ins, outs = refs[:peers], refs[peers:]
        for c in range(chans):
            whole = jnp.concatenate([r[c] for r in ins], axis=0)
            mixed = jnp.dot(mixer_ref[...], whole, preferred_element_type=F32).astype(BF16)
            for e in range(peers):
                outs[e][c] = mixed[e * hours : (e + 1) * hours]

    return pl.pallas_call(
        body,
        out_shape=[jax.ShapeDtypeStruct((chans, hours, rows), BF16)] * peers,
        in_specs=[VMEM] * (1 + peers),
        out_specs=[VMEM] * peers,
        compiler_params=limit(4),
        name="mix_hours",
    )(mixer, *pieces)


def in_order(places, pieces):
    peers = len(pieces)
    chans, hours, rows = pieces[0].shape

    def body(places_ref, *refs):
        out = refs[peers]
        for e in range(peers):
            out[pl.ds(places_ref[e] * chans, chans)] = refs[e][...]

    return pl.pallas_call(
        body,
        out_shape=jax.ShapeDtypeStruct((peers * chans, hours, rows), BF16),
        in_specs=[SMEM] + [VMEM] * peers,
        out_specs=VMEM,
        compiler_params=limit(4),
        name="in_order",
    )(places, *pieces)


def joined(refs, shape):
    out, at = [], 0
    for count in shape:
        parts = [r[...] for r in refs[at : at + count]]
        out.append(parts[0] if count == 1 else jnp.concatenate(parts, axis=0))
        at += count
    return out


def apply_kernel(ker_bf, parts, shape):
    total = len(parts)
    length = sum(p.shape[0] for p in parts[: shape[0]])
    width = parts[0].shape[1]

    def body(ker_ref, *refs):
        blocks = joined(refs[:total], shape)
        acc = None
        for q, block in enumerate(blocks):
            term = lax.dot_general(
                block,
                ker_ref[:, q * width : (q + 1) * width],
                (((1,), (1,)), ((), ())),
                preferred_element_type=F32,
            )
            acc = term if acc is None else acc + term
        refs[total][...] = acc[:, :width]
        refs[total + 1][...] = acc[:, width:].astype(BF16)

    return pl.pallas_call(
        body,
        out_shape=[
            jax.ShapeDtypeStruct((length, width), F32),
            jax.ShapeDtypeStruct((length, width), BF16),
        ],
        in_specs=[VMEM] * (1 + total),
        out_specs=[VMEM] * 2,
        compiler_params=limit(8),
        name="apply_kernel",
    )(ker_bf, *parts)


def add_gram(gram, field_rows, parts, shape):
    total = len(parts)
    sides = len(field_rows)
    first = gram is None
    width = parts[0].shape[1]
    height = field_rows[0].shape[0]
    lead = 0 if first else 1

    def body(*refs):
        out = refs[-1]
        blocks = joined(refs[lead + sides : lead + sides + total], shape)
        for s in range(sides):
            left = refs[lead + s][...]
            for q, block in enumerate(blocks):
                term = jnp.dot(left, block, preferred_element_type=F32)
                at = (slice(s * height, (s + 1) * height), slice(q * width, (q + 1) * width))
                out[at] = term if first else refs[0][at] + term

    args = ([] if first else [gram]) + list(field_rows) + list(parts)
    return pl.pallas_call(
        body,
        out_shape=jax.ShapeDtypeStruct((sides * height, len(shape) * width), F32),
        in_specs=[VMEM] * len(args),
        out_specs=VMEM,
        input_output_aliases={} if first else {0: 0},
        compiler_params=limit(8),
        name="add_gram",
    )(*args)


def exact_rows(emb):
    high = emb.astype(BF16)
    rest = emb - high.astype(F32)
    middle = rest.astype(BF16)
    low = (rest - middle.astype(F32)).astype(BF16)
    return jnp.concatenate([high, middle, low, jnp.ones(emb.shape, BF16)], axis=0)


def embed_parts(gram, ker, emb_rows, emb_cols, width):
    emb_width = emb_rows.shape[0]
    sides = emb_rows.shape[1] // width
    chips = emb_cols.shape[1] // width
    scale = 1.0 / emb_width

    def differences(sums, emb):
        total = sums[:emb_width] + sums[emb_width : 2 * emb_width]
        total = total + sums[2 * emb_width : 3 * emb_width]
        return (total - emb * sums[3 * emb_width : 3 * emb_width + 1]) * scale

    def body(gram_ref, ker_ref, rows_ref, cols_ref, *outs):
        weight = (gram_ref[...] * ker_ref[...]).astype(BF16)
        emb_r, emb_c = rows_ref[...], cols_ref[...]
        by_row = lax.dot_general(
            exact_rows(emb_c), weight, (((1,), (1,)), ((), ())), preferred_element_type=F32
        )
        by_row = differences(by_row, emb_r)
        by_col = jnp.dot(exact_rows(emb_r), weight, preferred_element_type=F32)
        by_col = differences(by_col, emb_c)
        outs[0][...] = by_row[:, :width] + by_col[:, :width]
        for s in range(1, sides):
            outs[s][...] = by_row[:, s * width : (s + 1) * width]
        for q in range(1, chips):
            outs[sides - 1 + q][...] = by_col[:, q * width : (q + 1) * width]

    count = sides + chips - 1
    return pl.pallas_call(
        body,
        out_shape=[jax.ShapeDtypeStruct((emb_width, width), F32)] * count,
        in_specs=[VMEM] * 4,
        out_specs=[VMEM] * count,
        compiler_params=limit(8),
        name="embed_parts",
    )(gram, ker, emb_rows, emb_cols)


def first_round(block, stations):
    bits = range((stations // 2 - 1).bit_length())
    return {0: [block]} | {1 << b: [flip(block, "st", stations, 2 << b)] for b in bits}


def other_rounds(parts_of, stations):
    chips = stations // 2
    rows = parts_of[0][0].shape[0]
    unit = 16
    parts_of = dict(parts_of)
    for q in sorted(range(1, chips), key=lambda v: (bin(v).count("1"), v)):
        if q in parts_of:
            continue
        bits = [b for b in range(q.bit_length()) if q >> b & 1]
        cuts = [rows // unit * a // len(bits) * unit for a in range(len(bits) + 1)]
        parts = []
        for a, b in enumerate(bits):
            source = parts_of[q ^ (1 << b)]
            source = source[0] if len(source) == 1 else jnp.concatenate(source, axis=0)
            parts.append(flip(source[cuts[a] : cuts[a + 1]], "st", stations, 2 << b))
        parts_of[q] = parts
    flat = [p for q in range(chips) for p in parts_of[q]]
    return flat, [len(parts_of[q]) for q in range(chips)]


def on_device(cotangent, field, temporal, embed):
    hours, chans, rows = cotangent.shape
    stations = lax.axis_size("st")
    peers = lax.axis_size("hr")
    chips = stations // 2
    here = lax.axis_index("hr")
    amplitude = 1.0 / math.sqrt(rows * stations)
    starts = [chans * sum(SPLIT[:k]) // sum(SPLIT) for k in range(CHUNKS + 1)]
    groups = [b - a for a, b in zip(starts, starts[1:])]

    across = [here ^ d for d in range(peers)]
    places = jnp.stack(across).astype(jnp.int32)

    mixer = jnp.concatenate(
        [lax.dynamic_slice_in_dim(temporal, b * hours, hours, 0) for b in across], axis=0
    )
    mixer = jnp.concatenate(
        [lax.dynamic_slice_in_dim(mixer, a * hours, hours, 1) for a in across], axis=1
    ).T

    def turned(source, k):
        part = source[:, starts[k] : starts[k + 1]]
        part = row_major(jnp.transpose(part, (1, 0, 2)))
        share = groups[k] // peers
        return [lax.dynamic_slice_in_dim(part, a * share, share, 0) for a in across]

    def exchange(pieces):
        return [p if d == 0 else flip(p, "hr", peers, d) for d, p in enumerate(pieces)]

    pieces = [turned(cotangent, 0)]
    rest = after(cotangent, pieces[0])
    pieces += [turned(rest, k) for k in range(1, CHUNKS)]
    sent = {k: exchange(pieces[k]) for k in range(CHUNKS)}

    own = after(embed, pieces[1])
    left = [own, flip(own, "st", stations, 1)]
    right = [own] + [flip(own, "st", stations, 2 * q) for q in range(1, chips)]
    ker, ker_bf, emb_rows, emb_cols = kernel_matrix(left, right, amplitude)

    def turned_field(source, k):
        part = source[:, starts[k] : starts[k + 1]]
        part = row_major(jnp.transpose(part, (2, 1, 0)).reshape(rows, groups[k] * hours))
        return [part, flip(part, "st", stations, 1)]

    source = after(field, right[1:])
    field_rows = [turned_field(source, k) for k in range(CHUNKS)]

    state = {"gram": None}
    blocks, outs = {}, {}

    def mix(k):
        mixed = mix_hours(mixer, sent[k])
        blocks[k] = exchange(mixed)

    def order(k):
        block = in_order(places, blocks[k]).reshape(groups[k] * hours, rows)
        blocks[k] = first_round(block, stations)

    def relay(k):
        blocks[k] = other_rounds(blocks[k], stations)

    def contract(k):
        parts, shape = blocks[k]
        state["gram"] = add_gram(state["gram"], field_rows[k], parts, shape)
        own, other = apply_kernel(ker_bf, parts, shape)
        other = flip(other, "st", stations, 1)
        total = (own + other.astype(F32)).astype(BF16).reshape(groups[k], hours, rows)
        outs[k] = jnp.transpose(total, (1, 0, 2))

    run = {"mix": mix, "order": order, "relay": relay, "contract": contract}
    for name, k in plan():
        run[name](k)
    field_grad = jnp.zeros(field.shape, BF16)
    for k in range(CHUNKS):
        field_grad = lax.dynamic_update_slice_in_dim(field_grad, outs[k], starts[k], 1)

    parts = embed_parts(state["gram"], ker, emb_rows, emb_cols, rows)
    part = parts[0] + flip(parts[1], "st", stations, 1)
    for q in range(1, chips):
        part = part + flip(parts[1 + q], "st", stations, 2 * q)
    embed_grad = part
    for d in range(1, peers):
        embed_grad = embed_grad + flip(part, "hr", peers, d)
    return (field_grad, embed_grad)


def plan():
    return [(name[:-1], int(name[-1])) for line in PLAN for name in line.split()]


def solution(mesh):
    return jax.shard_map(
        on_device,
        mesh=mesh,
        in_specs=(P("hr", None, "st"), P("hr", None, "st"), P(), P(None, "st")),
        out_specs=(P("hr", None, "st"), P(None, "st")),
        check_vma=False,
    )
```

```python
import math

import jax
import jax.numpy as jnp
from jax import lax
from jax.experimental import pallas as pl
from jax.experimental.layout import Layout, with_layout_constraint
from jax.experimental.pallas import tpu as pltpu
from jax.sharding import PartitionSpec as P


HIGHEST = lax.Precision.HIGHEST
BF16 = jnp.bfloat16
F32 = jnp.float32
SPLIT = (2, 2, 1, 2, 1)
CHUNKS = len(SPLIT)

VMEM = pl.BlockSpec(memory_space=pltpu.VMEM)
SMEM = pl.BlockSpec(memory_space=pltpu.SMEM)


def limit(mib):
    return pltpu.CompilerParams(vmem_limit_bytes=mib << 20)


def after(values, gate):
    return values if gate is None else lax.optimization_barrier((values, gate))[0]


def row_major(x):
    return with_layout_constraint(x, Layout(major_to_minor=tuple(range(x.ndim))))


def kernel_matrix(left, right, amplitude):
    emb_width, width = left[0].shape
    n_left, n_right = len(left), len(right)

    def body(*refs):
        rows = jnp.concatenate([r[...] for r in refs[:n_left]], axis=1)
        cols = jnp.concatenate([r[...] for r in refs[n_left : n_left + n_right]], axis=1)
        ker, ker_bf, rows_out, cols_out = refs[n_left + n_right :]
        rows_out[...] = rows
        cols_out[...] = cols
        rows_t = rows.T
        norm_rows = jnp.sum(rows_t * rows_t, axis=1, keepdims=True)
        norm_cols = jnp.sum(cols * cols, axis=0, keepdims=True)
        cross = jnp.dot(rows_t, cols, precision=HIGHEST, preferred_element_type=F32)
        distance = norm_rows + norm_cols - 2.0 * cross
        tile = jnp.exp(distance * (-0.5 / emb_width)) * amplitude
        ker[...] = tile
        ker_bf[...] = tile.astype(BF16)

    shape = (n_left * width, n_right * width)
    return pl.pallas_call(
        body,
        out_shape=[
            jax.ShapeDtypeStruct(shape, F32),
            jax.ShapeDtypeStruct(shape, BF16),
            jax.ShapeDtypeStruct((emb_width, shape[0]), F32),
            jax.ShapeDtypeStruct((emb_width, shape[1]), F32),
        ],
        in_specs=[VMEM] * (n_left + n_right),
        out_specs=[VMEM] * 4,
        compiler_params=limit(12),
        name="kernel_matrix",
    )(*left, *right)


def flip(x, axis, size, mask):
    return lax.ppermute(x, axis, [(i, i ^ mask) for i in range(size)])


def mix_hours(mixer, pieces):
    peers = len(pieces)
    chans, hours, rows = pieces[0].shape

    def body(mixer_ref, *refs):
        ins, outs = refs[:peers], refs[peers:]
        for c in range(chans):
            whole = jnp.concatenate([r[c] for r in ins], axis=0)
            mixed = jnp.dot(mixer_ref[...], whole, preferred_element_type=F32).astype(BF16)
            for e in range(peers):
                outs[e][c] = mixed[e * hours : (e + 1) * hours]

    return pl.pallas_call(
        body,
        out_shape=[jax.ShapeDtypeStruct((chans, hours, rows), BF16)] * peers,
        in_specs=[VMEM] * (1 + peers),
        out_specs=[VMEM] * peers,
        compiler_params=limit(4),
        name="mix_hours",
    )(mixer, *pieces)


def in_order(places, pieces):
    peers = len(pieces)
    chans, hours, rows = pieces[0].shape

    def body(places_ref, *refs):
        out = refs[peers]
        for e in range(peers):
            out[pl.ds(places_ref[e] * chans, chans)] = refs[e][...]

    return pl.pallas_call(
        body,
        out_shape=jax.ShapeDtypeStruct((peers * chans, hours, rows), BF16),
        in_specs=[SMEM] + [VMEM] * peers,
        out_specs=VMEM,
        compiler_params=limit(4),
        name="in_order",
    )(places, *pieces)


def joined(refs, shape):
    out, at = [], 0
    for count in shape:
        parts = [r[...] for r in refs[at : at + count]]
        out.append(parts[0] if count == 1 else jnp.concatenate(parts, axis=0))
        at += count
    return out


def apply_kernel(ker_bf, parts, shape):
    total = len(parts)
    length = sum(p.shape[0] for p in parts[: shape[0]])
    width = parts[0].shape[1]

    def body(ker_ref, *refs):
        blocks = joined(refs[:total], shape)
        acc = None
        for q, block in enumerate(blocks):
            term = lax.dot_general(
                block,
                ker_ref[:, q * width : (q + 1) * width],
                (((1,), (1,)), ((), ())),
                preferred_element_type=F32,
            )
            acc = term if acc is None else acc + term
        refs[total][...] = acc[:, :width]
        refs[total + 1][...] = acc[:, width:].astype(BF16)

    return pl.pallas_call(
        body,
        out_shape=[
            jax.ShapeDtypeStruct((length, width), F32),
            jax.ShapeDtypeStruct((length, width), BF16),
        ],
        in_specs=[VMEM] * (1 + total),
        out_specs=[VMEM] * 2,
        compiler_params=limit(8),
        name="apply_kernel",
    )(ker_bf, *parts)


def add_gram(gram, field_rows, parts, shape):
    total = len(parts)
    sides = len(field_rows)
    first = gram is None
    width = parts[0].shape[1]
    height = field_rows[0].shape[1]
    lead = 0 if first else 1

    def body(*refs):
        out = refs[-1]
        blocks = joined(refs[lead + sides : lead + sides + total], shape)
        for s in range(sides):
            left = refs[lead + s][...].T
            for q, block in enumerate(blocks):
                term = jnp.dot(left, block, preferred_element_type=F32)
                at = (slice(s * height, (s + 1) * height), slice(q * width, (q + 1) * width))
                out[at] = term if first else refs[0][at] + term

    args = ([] if first else [gram]) + list(field_rows) + list(parts)
    return pl.pallas_call(
        body,
        out_shape=jax.ShapeDtypeStruct((sides * height, len(shape) * width), F32),
        in_specs=[VMEM] * len(args),
        out_specs=VMEM,
        input_output_aliases={} if first else {0: 0},
        compiler_params=limit(8),
        name="add_gram",
    )(*args)


def exact_rows(emb):
    high = emb.astype(BF16)
    rest = emb - high.astype(F32)
    middle = rest.astype(BF16)
    low = (rest - middle.astype(F32)).astype(BF16)
    return jnp.concatenate([high, middle, low, jnp.ones(emb.shape, BF16)], axis=0)


def embed_parts(gram, ker, emb_rows, emb_cols, width):
    emb_width = emb_rows.shape[0]
    sides = emb_rows.shape[1] // width
    chips = emb_cols.shape[1] // width
    scale = 1.0 / emb_width

    def differences(sums, emb):
        total = sums[:emb_width] + sums[emb_width : 2 * emb_width]
        total = total + sums[2 * emb_width : 3 * emb_width]
        return (total - emb * sums[3 * emb_width : 3 * emb_width + 1]) * scale

    def body(gram_ref, ker_ref, rows_ref, cols_ref, *outs):
        weight = (gram_ref[...] * ker_ref[...]).astype(BF16)
        emb_r, emb_c = rows_ref[...], cols_ref[...]
        by_row = lax.dot_general(
            exact_rows(emb_c), weight, (((1,), (1,)), ((), ())), preferred_element_type=F32
        )
        by_row = differences(by_row, emb_r)
        by_col = jnp.dot(exact_rows(emb_r), weight, preferred_element_type=F32)
        by_col = differences(by_col, emb_c)
        outs[0][...] = by_row[:, :width] + by_col[:, :width]
        for s in range(1, sides):
            outs[s][...] = by_row[:, s * width : (s + 1) * width]
        for q in range(1, chips):
            outs[sides - 1 + q][...] = by_col[:, q * width : (q + 1) * width]

    count = sides + chips - 1
    return pl.pallas_call(
        body,
        out_shape=[jax.ShapeDtypeStruct((emb_width, width), F32)] * count,
        in_specs=[VMEM] * 4,
        out_specs=[VMEM] * count,
        compiler_params=limit(8),
        name="embed_parts",
    )(gram, ker, emb_rows, emb_cols)


def first_round(block, stations):
    bits = range((stations // 2 - 1).bit_length())
    return {0: [block]} | {1 << b: [flip(block, "st", stations, 2 << b)] for b in bits}


def other_rounds(parts_of, stations):
    chips = stations // 2
    rows = parts_of[0][0].shape[0]
    unit = 16
    parts_of = dict(parts_of)
    for q in sorted(range(1, chips), key=lambda v: (bin(v).count("1"), v)):
        if q in parts_of:
            continue
        bits = [b for b in range(q.bit_length()) if q >> b & 1]
        cuts = [rows // unit * a // len(bits) * unit for a in range(len(bits) + 1)]
        parts = []
        for a, b in enumerate(bits):
            source = parts_of[q ^ (1 << b)]
            source = source[0] if len(source) == 1 else jnp.concatenate(source, axis=0)
            parts.append(flip(source[cuts[a] : cuts[a + 1]], "st", stations, 2 << b))
        parts_of[q] = parts
    flat = [p for q in range(chips) for p in parts_of[q]]
    return flat, [len(parts_of[q]) for q in range(chips)]


def on_device(cotangent, field, temporal, embed):
    hours, chans, rows = cotangent.shape
    stations = lax.axis_size("st")
    peers = lax.axis_size("hr")
    chips = stations // 2
    here = lax.axis_index("hr")
    amplitude = 1.0 / math.sqrt(rows * stations)
    starts = [chans * sum(SPLIT[:k]) // sum(SPLIT) for k in range(CHUNKS + 1)]
    groups = [b - a for a, b in zip(starts, starts[1:])]

    across = [here ^ d for d in range(peers)]
    places = jnp.stack(across).astype(jnp.int32)

    mixer = jnp.concatenate(
        [lax.dynamic_slice_in_dim(temporal, b * hours, hours, 0) for b in across], axis=0
    )
    mixer = jnp.concatenate(
        [lax.dynamic_slice_in_dim(mixer, a * hours, hours, 1) for a in across], axis=1
    ).T

    def turned(source, k):
        part = source[:, starts[k] : starts[k + 1]]
        part = row_major(jnp.transpose(part, (1, 0, 2)))
        share = groups[k] // peers
        return [lax.dynamic_slice_in_dim(part, a * share, share, 0) for a in across]

    def exchange(pieces):
        return [p if d == 0 else flip(p, "hr", peers, d) for d, p in enumerate(pieces)]

    pieces = [turned(cotangent, 0)]
    rest = after(cotangent, pieces[0])
    pieces += [turned(rest, k) for k in range(1, CHUNKS)]
    sent = {k: exchange(pieces[k]) for k in range(CHUNKS)}

    own = after(embed, pieces[1])
    left = [own, flip(own, "st", stations, 1)]
    right = [own] + [flip(own, "st", stations, 2 * q) for q in range(1, chips)]
    ker, ker_bf, emb_rows, emb_cols = kernel_matrix(left, right, amplitude)

    source = after(field, right[1:])

    def turned_field(k):
        part = row_major(jnp.transpose(source[:, starts[k] : starts[k + 1]], (1, 0, 2)))
        part = part.reshape(groups[k] * hours, rows)
        return [part, flip(part, "st", stations, 1)]

    field_rows = [turned_field(k) for k in range(CHUNKS)]

    state = {"gram": None}
    blocks, outs = {}, {}

    def mix(k):
        mixed = mix_hours(mixer, sent[k])
        blocks[k] = exchange(mixed)

    def order(k):
        block = in_order(places, blocks[k]).reshape(groups[k] * hours, rows)
        blocks[k] = first_round(block, stations)

    def relay(k):
        blocks[k] = other_rounds(blocks[k], stations)

    def gram(k):
        state["gram"] = add_gram(state["gram"], field_rows[k], *blocks[k])

    def apply(k):
        own, other = apply_kernel(ker_bf, *blocks[k])
        other = flip(other, "st", stations, 1)
        total = (own + other.astype(F32)).astype(BF16).reshape(groups[k], hours, rows)
        outs[k] = jnp.transpose(total, (1, 0, 2))

    for step in (mix, order, relay, gram, apply):
        for k in range(CHUNKS):
            step(k)
    field_grad = jnp.zeros(field.shape, BF16)
    for k in range(CHUNKS):
        field_grad = lax.dynamic_update_slice_in_dim(field_grad, outs[k], starts[k], 1)

    parts = embed_parts(state["gram"], ker, emb_rows, emb_cols, rows)
    part = parts[0] + flip(parts[1], "st", stations, 1)
    for q in range(1, chips):
        part = part + flip(parts[1 + q], "st", stations, 2 * q)
    embed_grad = part
    for d in range(1, peers):
        embed_grad = embed_grad + flip(part, "hr", peers, d)
    return (field_grad, embed_grad)


def solution(mesh):
    return jax.shard_map(
        on_device,
        mesh=mesh,
        in_specs=(P("hr", None, "st"), P("hr", None, "st"), P(), P(None, "st")),
        out_specs=(P("hr", None, "st"), P(None, "st")),
        check_vma=False,
    )
```

```python
import math

import jax
import jax.numpy as jnp
from jax import lax
from jax.experimental import pallas as pl
from jax.experimental.layout import Layout, with_layout_constraint
from jax.experimental.pallas import tpu as pltpu
from jax.sharding import PartitionSpec as P


HIGHEST = lax.Precision.HIGHEST
BF16 = jnp.bfloat16
F32 = jnp.float32
SPLIT = (2, 2, 1, 1, 2)
LATE = 2
CHUNKS = len(SPLIT)
EARLY = CHUNKS - LATE

VMEM = pl.BlockSpec(memory_space=pltpu.VMEM)
SMEM = pl.BlockSpec(memory_space=pltpu.SMEM)


def limit(mib):
    return pltpu.CompilerParams(vmem_limit_bytes=mib << 20)


def after(values, gate):
    return values if gate is None else lax.optimization_barrier((values, gate))[0]


def row_major(x):
    return with_layout_constraint(x, Layout(major_to_minor=tuple(range(x.ndim))))


def kernel_matrix(left, right, amplitude):
    emb_width, width = left[0].shape
    n_left, n_right = len(left), len(right)

    def body(*refs):
        rows = jnp.concatenate([r[...] for r in refs[:n_left]], axis=1)
        cols = jnp.concatenate([r[...] for r in refs[n_left : n_left + n_right]], axis=1)
        ker, ker_bf, rows_out, cols_out = refs[n_left + n_right :]
        rows_out[...] = rows
        cols_out[...] = cols
        rows_t = rows.T
        norm_rows = jnp.sum(rows_t * rows_t, axis=1, keepdims=True)
        norm_cols = jnp.sum(cols * cols, axis=0, keepdims=True)
        cross = jnp.dot(rows_t, cols, precision=HIGHEST, preferred_element_type=F32)
        distance = norm_rows + norm_cols - 2.0 * cross
        tile = jnp.exp(distance * (-0.5 / emb_width)) * amplitude
        ker[...] = tile
        ker_bf[...] = tile.astype(BF16)

    shape = (n_left * width, n_right * width)
    return pl.pallas_call(
        body,
        out_shape=[
            jax.ShapeDtypeStruct(shape, F32),
            jax.ShapeDtypeStruct(shape, BF16),
            jax.ShapeDtypeStruct((emb_width, shape[0]), F32),
            jax.ShapeDtypeStruct((emb_width, shape[1]), F32),
        ],
        in_specs=[VMEM] * (n_left + n_right),
        out_specs=[VMEM] * 4,
        compiler_params=limit(12),
        name="kernel_matrix",
    )(*left, *right)


def flip(x, axis, size, mask):
    return lax.ppermute(x, axis, [(i, i ^ mask) for i in range(size)])


def mixer_matrix(places, temporal):
    peers = places.shape[0]
    hours = temporal.shape[0] // peers

    def body(places_ref, temporal_ref, out, turned):
        def block(ref, d):
            return ref[pl.ds(pl.multiple_of(places_ref[d] * hours, hours), hours), :]

        whole = jnp.concatenate([block(temporal_ref, d) for d in range(peers)], axis=0)
        turned[...] = whole.T
        for e in range(peers):
            out[e * hours : (e + 1) * hours, :] = block(turned, e)

    return pl.pallas_call(
        body,
        out_shape=jax.ShapeDtypeStruct(temporal.shape, BF16),
        in_specs=[SMEM, VMEM],
        out_specs=VMEM,
        scratch_shapes=[pltpu.VMEM(temporal.shape, BF16)],
        compiler_params=limit(4),
        name="mixer_matrix",
    )(places, temporal)


def mix_hours(mixer, pieces):
    peers = len(pieces)
    chans, hours, rows = pieces[0].shape

    def body(mixer_ref, *refs):
        ins, outs = refs[:peers], refs[peers:]
        for c in range(chans):
            whole = jnp.concatenate([r[c] for r in ins], axis=0)
            mixed = jnp.dot(mixer_ref[...], whole, preferred_element_type=F32).astype(BF16)
            for e in range(peers):
                outs[e][c] = mixed[e * hours : (e + 1) * hours]

    return pl.pallas_call(
        body,
        out_shape=[jax.ShapeDtypeStruct((chans, hours, rows), BF16)] * peers,
        in_specs=[VMEM] * (1 + peers),
        out_specs=[VMEM] * peers,
        compiler_params=limit(4),
        name="mix_hours",
    )(mixer, *pieces)


def in_order(places, pieces):
    peers = len(pieces)
    chans, hours, rows = pieces[0].shape

    def body(places_ref, *refs):
        out = refs[peers]
        for e in range(peers):
            out[pl.ds(places_ref[e] * chans, chans)] = refs[e][...]

    return pl.pallas_call(
        body,
        out_shape=jax.ShapeDtypeStruct((peers * chans, hours, rows), BF16),
        in_specs=[SMEM] + [VMEM] * peers,
        out_specs=VMEM,
        compiler_params=limit(4),
        name="in_order",
    )(places, *pieces)


def joined(refs, shape):
    out, at = [], 0
    for count in shape:
        parts = [r[...] for r in refs[at : at + count]]
        out.append(parts[0] if count == 1 else jnp.concatenate(parts, axis=0))
        at += count
    return out


def apply_kernel(ker_bf, parts, shape):
    total = len(parts)
    length = sum(p.shape[0] for p in parts[: shape[0]])
    width = parts[0].shape[1]

    def body(ker_ref, *refs):
        blocks = joined(refs[:total], shape)
        acc = None
        for q, block in enumerate(blocks):
            term = lax.dot_general(
                block,
                ker_ref[:, q * width : (q + 1) * width],
                (((1,), (1,)), ((), ())),
                preferred_element_type=F32,
            )
            acc = term if acc is None else acc + term
        refs[total][...] = acc[:, :width]
        refs[total + 1][...] = acc[:, width:].astype(BF16)

    return pl.pallas_call(
        body,
        out_shape=[
            jax.ShapeDtypeStruct((length, width), F32),
            jax.ShapeDtypeStruct((length, width), BF16),
        ],
        in_specs=[VMEM] * (1 + total),
        out_specs=[VMEM] * 2,
        compiler_params=limit(8),
        name="apply_kernel",
    )(ker_bf, *parts)


def add_gram(gram, sides, parts, shape):
    total = len(parts)
    first = gram is None
    width = parts[0].shape[1]
    height = sides[0][0][0].shape[1]
    lead = 0 if first else 1
    lefts = [piece[0] for side in sides for piece in side]

    def body(*refs):
        out = refs[-1]
        at = lead
        blocks = joined(refs[lead + len(lefts) : lead + len(lefts) + total], shape)
        for s, side in enumerate(sides):
            pieces = [refs[at + n][low:high, :] for n, (_, low, high) in enumerate(side)]
            at += len(side)
            left = pieces[0] if len(pieces) == 1 else jnp.concatenate(pieces, axis=0)
            left = left.T
            for q, block in enumerate(blocks):
                term = jnp.dot(left, block, preferred_element_type=F32)
                here = (slice(s * height, (s + 1) * height), slice(q * width, (q + 1) * width))
                out[here] = term if first else refs[0][here] + term

    args = ([] if first else [gram]) + lefts + list(parts)
    return pl.pallas_call(
        body,
        out_shape=jax.ShapeDtypeStruct((len(sides) * height, len(shape) * width), F32),
        in_specs=[VMEM] * len(args),
        out_specs=VMEM,
        input_output_aliases={} if first else {0: 0},
        compiler_params=limit(12),
        name="add_gram",
    )(*args)


def exact_rows(emb):
    high = emb.astype(BF16)
    rest = emb - high.astype(F32)
    middle = rest.astype(BF16)
    low = (rest - middle.astype(F32)).astype(BF16)
    return jnp.concatenate([high, middle, low, jnp.ones(emb.shape, BF16)], axis=0)


def embed_parts(gram, ker, emb_rows, emb_cols, width):
    emb_width = emb_rows.shape[0]
    sides = emb_rows.shape[1] // width
    chips = emb_cols.shape[1] // width
    scale = 1.0 / emb_width

    def differences(sums, emb):
        total = sums[:emb_width] + sums[emb_width : 2 * emb_width]
        total = total + sums[2 * emb_width : 3 * emb_width]
        return (total - emb * sums[3 * emb_width : 3 * emb_width + 1]) * scale

    def body(gram_ref, ker_ref, rows_ref, cols_ref, *outs):
        weight = (gram_ref[...] * ker_ref[...]).astype(BF16)
        emb_r, emb_c = rows_ref[...], cols_ref[...]
        by_row = lax.dot_general(
            exact_rows(emb_c), weight, (((1,), (1,)), ((), ())), preferred_element_type=F32
        )
        by_row = differences(by_row, emb_r)
        by_col = jnp.dot(exact_rows(emb_r), weight, preferred_element_type=F32)
        by_col = differences(by_col, emb_c)
        outs[0][...] = by_row[:, :width] + by_col[:, :width]
        for s in range(1, sides):
            outs[s][...] = by_row[:, s * width : (s + 1) * width]
        for q in range(1, chips):
            outs[sides - 1 + q][...] = by_col[:, q * width : (q + 1) * width]

    count = sides + chips - 1
    return pl.pallas_call(
        body,
        out_shape=[jax.ShapeDtypeStruct((emb_width, width), F32)] * count,
        in_specs=[VMEM] * 4,
        out_specs=[VMEM] * count,
        compiler_params=limit(8),
        name="embed_parts",
    )(gram, ker, emb_rows, emb_cols)


def first_round(block, stations):
    bits = range((stations // 2 - 1).bit_length())
    return {0: [block]} | {1 << b: [flip(block, "st", stations, 2 << b)] for b in bits}


def other_rounds(parts_of, stations):
    chips = stations // 2
    rows = parts_of[0][0].shape[0]
    unit = 16
    parts_of = dict(parts_of)
    for q in sorted(range(1, chips), key=lambda v: (bin(v).count("1"), v)):
        if q in parts_of:
            continue
        bits = [b for b in range(q.bit_length()) if q >> b & 1]
        cuts = [rows // unit * a // len(bits) * unit for a in range(len(bits) + 1)]
        parts = []
        for a, b in enumerate(bits):
            source = parts_of[q ^ (1 << b)]
            source = source[0] if len(source) == 1 else jnp.concatenate(source, axis=0)
            parts.append(flip(source[cuts[a] : cuts[a + 1]], "st", stations, 2 << b))
        parts_of[q] = parts
    flat = [p for q in range(chips) for p in parts_of[q]]
    return flat, [len(parts_of[q]) for q in range(chips)]


def on_device(cotangent, field, temporal, embed):
    hours, chans, rows = cotangent.shape
    stations = lax.axis_size("st")
    peers = lax.axis_size("hr")
    chips = stations // 2
    here = lax.axis_index("hr")
    amplitude = 1.0 / math.sqrt(rows * stations)
    starts = [chans * sum(SPLIT[:k]) // sum(SPLIT) for k in range(CHUNKS + 1)]
    groups = [b - a for a, b in zip(starts, starts[1:])]

    across = [here ^ d for d in range(peers)]
    places = jnp.stack(across).astype(jnp.int32)

    mixer = mixer_matrix(places, temporal)

    def turned(source, k):
        part = source[:, starts[k] : starts[k + 1]]
        part = row_major(jnp.transpose(part, (1, 0, 2)))
        share = groups[k] // peers
        return [lax.dynamic_slice_in_dim(part, a * share, share, 0) for a in across]

    def exchange(pieces):
        return [p if d == 0 else flip(p, "hr", peers, d) for d, p in enumerate(pieces)]

    pieces = [turned(cotangent, 0)]
    rest = after(cotangent, pieces[0])
    pieces += [turned(rest, k) for k in range(1, CHUNKS)]
    sent = {k: exchange(pieces[k]) for k in range(CHUNKS)}

    own = after(embed, pieces[1])
    left = [own, flip(own, "st", stations, 1)]
    right = [own] + [flip(own, "st", stations, 2 * q) for q in range(1, chips)]
    ker, ker_bf, emb_rows, emb_cols = kernel_matrix(left, right, amplitude)

    source = after(field, right[1:])

    def turned_field(low, high):
        part = row_major(jnp.transpose(source[:, low:high], (1, 0, 2)))
        return part.reshape((high - low) * hours, rows)

    field_early = turned_field(0, starts[EARLY])
    field_early = [field_early, flip(field_early, "st", stations, 1)]
    field_late = turned_field(starts[EARLY], chans)
    field_late = first_round(field_late, stations)
    field_late = other_rounds(field_late, stations)

    state = {"gram": None}
    blocks, outs, late = {}, {}, {}

    def mix(k):
        mixed = mix_hours(mixer, sent[k])
        blocks[k] = exchange(mixed)

    def order(k):
        block = in_order(places, blocks[k]).reshape(groups[k] * hours, rows)
        blocks[k] = first_round(block, stations)
        if k >= EARLY:
            late[k] = [block, flip(block, "st", stations, 1)]

    def relay(k):
        blocks[k] = other_rounds(blocks[k], stations)

    def gram(k):
        low, high = starts[k] * hours, starts[k + 1] * hours
        sides = [[(side, low, high)] for side in field_early]
        state["gram"] = add_gram(state["gram"], sides, *blocks[k])

    def apply(k):
        own, other = apply_kernel(ker_bf, *blocks[k])
        other = flip(other, "st", stations, 1)
        total = (own + other.astype(F32)).astype(BF16).reshape(groups[k], hours, rows)
        outs[k] = jnp.transpose(total, (1, 0, 2))

    for step in (mix, order, relay, gram, apply):
        for k in range(EARLY if step is gram else CHUNKS):
            step(k)
    sides = [[(late[k][s], 0, late[k][s].shape[0]) for k in sorted(late)] for s in range(2)]
    state["gram"] = add_gram(state["gram"], sides, *field_late)
    field_grad = jnp.zeros(field.shape, BF16)
    for k in range(CHUNKS):
        field_grad = lax.dynamic_update_slice_in_dim(field_grad, outs[k], starts[k], 1)

    parts = embed_parts(state["gram"], ker, emb_rows, emb_cols, rows)
    others = [flip(parts[1], "st", stations, 1)]
    others += [flip(parts[1 + q], "st", stations, 2 * q) for q in range(1, chips)]
    part = parts[0]
    for other in others:
        part = part + other
    others = [flip(part, "hr", peers, d) for d in range(1, peers)]
    embed_grad = part
    for other in others:
        embed_grad = embed_grad + other
    return (field_grad, embed_grad)


def solution(mesh):
    return jax.shard_map(
        on_device,
        mesh=mesh,
        in_specs=(P("hr", None, "st"), P("hr", None, "st"), P(), P(None, "st")),
        out_specs=(P("hr", None, "st"), P(None, "st")),
        check_vma=False,
    )
```
